256 devices in a mesh: feat: 32 (over z, x), blk: 8 (over y, core).
Axes of the slice: x: 4, y: 4, z: 8, core: 2. Of those that a mesh axis runs over, the one named last changes fastest.
Arguments:
- features: bfloat16 [1024, 32, 8192], P('feat', None, 'blk'), may hold values from -6 to 6
- adj_local: bfloat16 [262144, 1024], P(('feat', 'blk')), may hold values from 0.049804688 to 1
- adj_remote: bfloat16 [262144, 1792], P(('feat', 'blk')), may hold values from 0.049804688 to 1
- tile_mask: int32 [2048, 22], P(('feat', 'blk')), may hold values from 0 to 1, as said below
- w_self: bfloat16 [1024, 256], replicated, may hold values from -0.1875 to 0.1875
- w_neigh: bfloat16 [1024, 256], replicated, may hold values from -0.1875 to 0.1875
- out_bias: float32 [256], replicated, may hold values from -4 to 4
Outputs:
- hidden_out: bfloat16 [262144, 256], P(('feat', 'blk'))
The draws below stay inside these ranges and needn't reach their ends.
Inputs may be any that keep to these rules, and one draw needn't show every extreme that they name: `tile_mask`: 0 or 1 for each tile; the 128 x 128 tiles on the diagonal of every node's adj_local block are 1.
All inputs are finite; a program needn't handle non-finite values.
Results may differ from the reference program's by a relative error of at most 0.0035.
Values may be sent and summed in bfloat16 or wider, within the bound.
No kernel may reach another device: no remote copies, remote signals or barrier semaphores. Data moves between devices by JAX's collectives and lax.ppermute only.
A program may use at most 128 MiB of HBM per device.

```python
import jax
import jax.numpy as jnp
from jax import lax

F = 1024
HID = 256
TILE = 128
NB = 1024
HALO = 256
NODES = 262144
N_FEAT = 32
N_BLK = 8


def draw_tile_mask(key, part):
    tile_rows = NODES // TILE
    tile_cols = (NB + (N_BLK - 1) * HALO) // TILE
    per_device = NB // TILE
    device_count = tile_rows // per_device
    key_level = jax.random.fold_in(key, 11)
    key_tiles = jax.random.fold_in(key, 23)
    dense_device = jax.random.randint(key_level, (device_count,), 0, 4) == 0
    density = jnp.where(dense_device, 16, 1)
    density_rows = jnp.repeat(density, per_device)
    uniform_level = jax.random.randint(key_tiles, (tile_rows, tile_cols), 0, 16)
    alive_tile = uniform_level < density_rows[:, None]
    row_pos = jnp.arange(tile_rows) % per_device
    col_pos = jnp.arange(tile_cols)
    on_diagonal = row_pos[:, None] == col_pos[None, :]
    return jnp.where(alive_tile | on_diagonal, 1, 0).astype(jnp.int32)


def levels(stream_key, dims, shards, smallest, top_value):
    level = 1.0
    for dim, shards_of in shards:
        heights = jax.random.uniform(jax.random.fold_in(jax.random.fold_in(stream_key, 6), dim), (shards_of,), jnp.float32, smallest / len(shards), top_value / len(shards))
        level = level * jnp.repeat(jnp.exp(heights), dims[dim] // shards_of).reshape((-1,) + (1,) * (len(dims) - 1 - dim))
    return level


def noise(stream_key, dims, spread, most, shards=(), kind=jnp.bfloat16):
    array = jax.random.normal(stream_key, dims, jnp.float32) * spread
    if len(shards) > 0:
        array = levels(stream_key, dims, shards, -0.22, 0.18) * array
    return jnp.clip(array, min=-most, max=most).astype(kind)


def setup_inputs(seed: int = 0) -> dict:
    splits = jax.random.split(jax.random.key(seed), 8)
    features = noise(splits[0], (F, N_FEAT, N_BLK * NB), 1.0, 6.0, ((0, 32), (2, 8)))
    adj_local = jnp.clip(0.049804688 + 0.9501953 * jax.random.uniform(splits[1], (NODES, NB), jnp.float32) ** levels(splits[1], (NODES, NB), ((0, 256),), -0.2, 0.2), 0.049804688, 1.0).astype(jnp.bfloat16)
    adj_remote = jnp.clip(0.049804688 + 0.9501953 * jax.random.uniform(splits[2], (NODES, (N_BLK - 1) * HALO), jnp.float32) ** levels(splits[2], (NODES, (N_BLK - 1) * HALO), ((0, 256),), -0.2, 0.2), 0.049804688, 1.0).astype(jnp.bfloat16)
    tile_mask = draw_tile_mask(jax.random.fold_in(splits[7], 71), 0)
    w_self = noise(splits[4], (F, HID), F ** -0.5, 0.1875)
    w_neigh = noise(splits[5], (F, HID), F ** -0.5, 0.1875)
    out_bias = noise(splits[6], (HID,), 1.0, 4.0, (), jnp.float32)
    return dict(features=features, adj_local=adj_local, adj_remote=adj_remote, tile_mask=tile_mask, w_self=w_self, w_neigh=w_neigh, out_bias=out_bias)


def expand_tiles(adjacency, tile_flags):
    row_total, col_total = adjacency.shape
    blocked = adjacency.reshape(row_total // TILE, TILE, col_total // TILE, TILE)
    blocked = blocked * tile_flags.astype(jnp.bfloat16)[:, None, :, None]
    return blocked.reshape(row_total, col_total)

def reference(features, adj_local, adj_remote, tile_mask, w_self, w_neigh, out_bias):
    local_tiles = NB // TILE
    zero_index = jnp.zeros((), jnp.int32)
    wide_neigh = w_neigh.astype(jnp.float32)

    def one_block(block_id):
        group_id = (block_id // N_BLK).astype(jnp.int32)
        block_pos = (block_id % N_BLK).astype(jnp.int32)
        own_feats = lax.dynamic_slice(features, (zero_index, group_id, (block_pos * NB).astype(jnp.int32)), (F, 1, NB)).reshape(F, NB)
        row_start = (block_id * NB).astype(jnp.int32)
        tile_start = (block_id * local_tiles).astype(jnp.int32)
        tile_flags = lax.dynamic_slice_in_dim(tile_mask, tile_start, local_tiles, 0)
        live_local = expand_tiles(lax.dynamic_slice_in_dim(adj_local, row_start, NB, 0), tile_flags[:, :local_tiles])
        live_remote = expand_tiles(lax.dynamic_slice_in_dim(adj_remote, row_start, NB, 0), tile_flags[:, local_tiles:])
        degree = lax.optimization_barrier(jnp.sum(live_local.astype(jnp.float32), axis=1)) + lax.optimization_barrier(jnp.sum(live_remote.astype(jnp.float32), axis=1))
        summed = jnp.dot(live_local, own_feats.T, preferred_element_type=jnp.float32)
        for offset in range(1, N_BLK):
            source = ((block_pos + (N_BLK - offset)) % N_BLK).astype(jnp.int32)
            halo_panel = lax.dynamic_slice(features, (zero_index, group_id, (source * NB).astype(jnp.int32)), (F, 1, HALO)).reshape(F, HALO)
            weight_piece = live_remote[:, (offset - 1) * HALO:offset * HALO]
            summed = summed + jnp.dot(weight_piece, halo_panel.T, preferred_element_type=jnp.float32)
        neigh_term = jnp.dot(summed, wide_neigh, precision=lax.Precision.HIGHEST) / jnp.sqrt(degree)[:, None]
        self_term = jnp.dot(own_feats.T, w_self, preferred_element_type=jnp.float32)
        return jax.nn.relu(self_term + neigh_term + out_bias[None, :]).astype(jnp.bfloat16)
    blocks = lax.map(one_block, jnp.arange(N_FEAT * N_BLK, dtype=jnp.int32))
    return blocks.reshape(NODES, HID)
```

```python
import jax
import jax.numpy as jnp
from jax import lax
from jax.experimental import pallas as pl
from jax.experimental.pallas import tpu as pltpu
from jax.sharding import PartitionSpec as P

TILE = 128
NZ = 8
NX = 4
BF = jnp.bfloat16
F32 = jnp.float32


VM = pltpu.CompilerParams(vmem_limit_bytes=16 << 20)


def full(shape):
    return pl.BlockSpec(shape, lambda *_: (0,) * len(shape))


def feat_shift(dz, dx):
    return [
        (z * NX + x, (z + dz) % NZ * NX + (x + dx) % NX) for z in range(NZ) for x in range(NX)
    ]


def blk_shift(dy, dc):
    return [(y * 2 + c, (y + dy) % 4 * 2 + (c + dc) % 2) for y in range(4) for c in range(2)]


def head_kernel(me_ref, x_ref, *rest):
    outs, turned = rest[:-1], rest[-1]
    turned[...] = jnp.swapaxes(x_ref[...], 0, 1)
    z, x = me_ref[0] // NX, me_ref[0] % NX
    for dz in range(NZ):
        for j in range(NX):
            outs[dz][j] = turned[(z + dz) % NZ * NX + (x + j) % NX]


def split_head(me, features, halo):
    f, g, _ = features.shape
    return pl.pallas_call(
        head_kernel,
        grid_spec=pltpu.PrefetchScalarGridSpec(
            num_scalar_prefetch=1,
            grid=(1,),
            in_specs=[full((f, g, halo))],
            out_specs=[full((NX, f, halo))] * NZ,
            scratch_shapes=[pltpu.VMEM((g, f, halo), BF)],
        ),
        out_shape=[jax.ShapeDtypeStruct((NX, f, halo), BF)] * NZ,
        compiler_params=VM,
        name="split_head",
    )(me, features)


def tail_kernel(x_ref, o_ref):
    o_ref[...] = jnp.swapaxes(x_ref[...], 0, 1)


def split_tail(features, halo):
    f, g, n = features.shape
    return pl.pallas_call(
        tail_kernel,
        grid=(n // halo - 1,),
        in_specs=[pl.BlockSpec((f, g, halo), lambda i: (0, 0, i + 1))],
        out_specs=pl.BlockSpec((g, f, halo), lambda i: (0, 0, i)),
        out_shape=jax.ShapeDtypeStruct((g, f, n - halo), BF),
        compiler_params=VM,
        name="split_tail",
    )(features)


def regroup_kernel(*refs):
    ins, outs = refs[:NZ], refs[NZ:]
    f = ins[0].shape[1]
    for j in range(NX):
        for dz in range(NZ):
            outs[j][dz * f : (dz + 1) * f, :] = ins[dz][j]


def regroup(parts):
    _, f, halo = parts[0].shape
    return pl.pallas_call(
        regroup_kernel,
        grid=(1,),
        in_specs=[full((NX, f, halo))] * NZ,
        out_specs=[full((NZ * f, halo))] * NX,
        out_shape=[jax.ShapeDtypeStruct((NZ * f, halo), BF)] * NX,
        compiler_params=VM,
        name="regroup",
    )(*parts)


def halo_kernel(me_ref, a, b, c, d, ws_ref, wn_ref, self_ref, h_ref, w_ref):
    z, x = me_ref[0] // NX, me_ref[0] % NX
    rows, hid = a.shape[0], ws_ref.shape[1]
    f = rows // NZ
    total = None
    for j, part in enumerate((a, b, c, d)):
        for dz in range(NZ):
            src = ((z + (NZ - dz)) % NZ * NX + (x + (NX - j)) % NX) * f
            src = pl.multiple_of(src, f)
            w_ref[dz * f : (dz + 1) * f, :hid] = ws_ref[pl.ds(src, f), :]
            w_ref[dz * f : (dz + 1) * f, hid:] = wn_ref[pl.ds(src, f), :]
        one = lax.dot_general(
            part[...], w_ref[...], (((0,), (0,)), ((), ())), preferred_element_type=F32
        )
        total = one if total is None else total + one
    self_ref[...] = total[:, :hid]
    h = total[:, hid:]
    high = h.astype(BF)
    h_ref[:, :hid] = high
    h_ref[:, hid:] = (h - high.astype(F32)).astype(BF)


def halo_hidden(me, parts, w_self, w_neigh):
    rows, halo = parts[0].shape
    total, hid = w_self.shape
    return pl.pallas_call(
        halo_kernel,
        grid_spec=pltpu.PrefetchScalarGridSpec(
            num_scalar_prefetch=1,
            grid=(1,),
            in_specs=[full((rows, halo))] * NX + [full((total, hid))] * 2,
            out_specs=[full((halo, hid)), full((halo, 2 * hid))],
            scratch_shapes=[pltpu.VMEM((rows, 2 * hid), BF)],
        ),
        out_shape=[
            jax.ShapeDtypeStruct((halo, hid), F32),
            jax.ShapeDtypeStruct((halo, 2 * hid), BF),
        ],
        compiler_params=VM,
        name="halo_hidden",
    )(me, *parts, w_self, w_neigh)


def mask_kernel(mask_ref, al_ref, ar_ref, head_ref, tail_ref, remote_ref, scale_ref):
    row = pl.program_id(0)
    local, halo = al_ref.shape[1] // TILE, head_ref.shape[1]
    degree = jnp.zeros((TILE, TILE), F32)
    for t in range(local + ar_ref.shape[1] // TILE):
        flag = mask_ref[row, t].astype(F32)
        if t < local:
            at = t * TILE
            tile = al_ref[:, at : at + TILE].astype(F32) * flag
            if at < halo:
                head_ref[:, at : at + TILE] = tile.astype(BF)
            else:
                tail_ref[:, at - halo : at - halo + TILE] = tile.astype(BF)
        else:
            at = (t - local) * TILE
            tile = ar_ref[:, at : at + TILE].astype(F32) * flag
            remote_ref[:, at : at + TILE] = tile.astype(BF)
        degree = degree + tile
    whole = jnp.sum(degree, axis=1, keepdims=True)
    scale_ref[...] = jnp.broadcast_to(1.0 / jnp.sqrt(whole), (TILE, TILE))


def mask_tiles(tile_mask, adj_local, adj_remote, halo):
    rows, n = adj_local.shape
    r = adj_remote.shape[1]
    line = lambda w: pl.BlockSpec((TILE, w), lambda i, _: (i, 0))
    return pl.pallas_call(
        mask_kernel,
        grid_spec=pltpu.PrefetchScalarGridSpec(
            num_scalar_prefetch=1,
            grid=(rows // TILE,),
            in_specs=[line(n), line(r)],
            out_specs=[line(halo), line(n - halo), line(r), line(TILE)],
        ),
        out_shape=[
            jax.ShapeDtypeStruct((rows, halo), BF),
            jax.ShapeDtypeStruct((rows, n - halo), BF),
            jax.ShapeDtypeStruct((rows, r), BF),
            jax.ShapeDtypeStruct((rows, TILE), F32),
        ],
        compiler_params=VM,
        name="mask_tiles",
    )(tile_mask, adj_local, adj_remote)


def gather_kernel(core_ref, head_ref, remote_ref, *rest):
    slots, o_ref = rest[:-1], rest[-1]
    core = core_ref[0]
    halo, hid = slots[0].shape[0], o_ref.shape[1]
    total = jnp.dot(head_ref[...], slots[0][...], preferred_element_type=F32)
    for s in range(1, len(slots)):
        dy = s if s < 4 else s - 4
        column = 2 * dy - 1 if s < 4 else (2 * dy + 2 * core + 7) % 8 - 1
        at = column * halo if s < 4 else pl.multiple_of(column * halo, halo)
        total = total + jnp.dot(
            remote_ref[:, pl.ds(at, halo)], slots[s][...], preferred_element_type=F32
        )
    o_ref[...] = total[:, :hid] + total[:, hid:]


def gather_halo(core, head, remote, slots):
    rows, halo = head.shape
    hid = slots[0].shape[1] // 2
    block = 256
    line = lambda w: pl.BlockSpec((block, w), lambda i, _: (i, 0))
    return pl.pallas_call(
        gather_kernel,
        grid_spec=pltpu.PrefetchScalarGridSpec(
            num_scalar_prefetch=1,
            grid=(rows // block,),
            in_specs=[line(halo), line(remote.shape[1])] + [full((halo, 2 * hid))] * len(slots),
            out_specs=line(hid),
        ),
        out_shape=jax.ShapeDtypeStruct((rows, hid), F32),
        compiler_params=VM,
        name="gather_halo",
    )(core, head, remote, *slots)


def last_kernel(x_ref, ws_ref, wn_ref, tail_ref, acc_ref, scale_ref, sh_ref, bias_ref, o_ref, h_ref, s_ref):
    halo, hid = sh_ref.shape
    first = (((0,), (0,)), ((), ()))
    s_ref[:halo, :] = sh_ref[...]
    s_ref[halo:, :] = lax.dot_general(x_ref[...], ws_ref[...], first, preferred_element_type=F32)
    h = lax.dot_general(x_ref[...], wn_ref[...], first, preferred_element_type=F32)
    high = h.astype(BF)
    h_ref[:, :hid] = high
    h_ref[:, hid:] = (h - high.astype(F32)).astype(BF)
    rows, block = o_ref.shape[0], 256
    for i in range(0, rows, block):
        at = slice(i, i + block)
        both = jnp.dot(tail_ref[at, :], h_ref[...], preferred_element_type=F32)
        summed = acc_ref[at, :] + both[:, :hid] + both[:, hid:]
        scale = jnp.concatenate([scale_ref[at, :]] * (hid // TILE), axis=1)
        o_ref[at, :] = jnp.maximum(s_ref[at, :] + summed * scale + bias_ref[...], 0.0).astype(BF)


def last_step(x, w_self, w_neigh, tail, acc, scale, self_head, bias):
    rows, hid = acc.shape
    args = (x, w_self, w_neigh, tail, acc, scale, self_head, bias)
    return pl.pallas_call(
        last_kernel,
        grid=(1,),
        in_specs=[full(a.shape) for a in args],
        out_specs=full((rows, hid)),
        scratch_shapes=[pltpu.VMEM((x.shape[1], 2 * hid), BF), pltpu.VMEM((rows, hid), F32)],
        out_shape=jax.ShapeDtypeStruct((rows, hid), BF),
        compiler_params=VM,
        name="last_step",
    )(*args)


def shards(features, adj_local, adj_remote, tile_mask, w_self, w_neigh, out_bias):
    halo = adj_remote.shape[1] // (lax.axis_size("blk") - 1)
    me = lax.axis_index("feat").reshape(1)
    core = (lax.axis_index("blk") % 2).reshape(1)

    head = split_head(me, features, halo)
    landed = [head[0]]
    for dz in range(1, NZ):
        landed.append(lax.ppermute(head[dz], "feat", feat_shift(dz, 0)))
    rest = split_tail(features, halo)
    rest = lax.all_to_all(rest, "feat", split_axis=0, concat_axis=0, tiled=True)
    rest = rest.reshape(-1, rest.shape[-1])

    live_head, live_tail, live_remote, scale = mask_tiles(tile_mask, adj_local, adj_remote, halo)
    rows = regroup(landed)
    parts = [rows[0]] + [lax.ppermute(rows[j], "feat", feat_shift(0, j)) for j in (1, 2, 3)]
    self_head, h_head = halo_hidden(me, parts, w_self, w_neigh)
    same = [h_head] + [lax.ppermute(h_head, "blk", blk_shift(dy, 0)) for dy in (1, 2, 3)]
    other = [lax.ppermute(h, "blk", blk_shift(0, 1)) for h in same]
    acc = gather_halo(core, live_head, live_remote, same + other)
    return last_step(
        rest, w_self, w_neigh, live_tail, acc, scale, self_head, out_bias[None, :]
    )


def solution(mesh):
    placed = (
        P("feat", None, "blk"),
        P(("feat", "blk"), None),
        P(("feat", "blk"), None),
        P(("feat", "blk"), None),
        P(),
        P(),
        P(),
    )

    return jax.shard_map(
        shards, mesh=mesh, in_specs=placed, out_specs=P(("feat", "blk"), None), check_vma=False
    )
```

```python
import jax
import jax.numpy as jnp
from jax import lax
from jax.experimental import pallas as pl
from jax.experimental.pallas import tpu as pltpu
from jax.sharding import PartitionSpec as P

TILE = 128
NZ = 8
NX = 4
NB = 8
BF = jnp.bfloat16
F32 = jnp.float32


VM = pltpu.CompilerParams(vmem_limit_bytes=16 << 20)


def full(shape):
    return pl.BlockSpec(shape, lambda *_: (0,) * len(shape))


def feat_shift(dz, dx):
    return [
        (z * NX + x, (z + dz) % NZ * NX + (x + dx) % NX) for z in range(NZ) for x in range(NX)
    ]


def blk_shift(dy, dc):
    return [(y * 2 + c, (y + dy) % 4 * 2 + (c + dc) % 2) for y in range(4) for c in range(2)]


def place(me_ref):
    feat = me_ref[0] // NB
    return feat // NX, feat % NX


def in_hbm(x):
    return pltpu.with_memory_space_constraint(x, pltpu.HBM)


def hbm(shape, dtype):
    return pltpu.HBM(shape, dtype)


def head_kernel(me_ref, x_ref, *rest):
    outs, turned = rest[:-1], rest[-1]
    turned[...] = jnp.swapaxes(x_ref[...], 0, 1)
    z, x = place(me_ref)
    for dz in range(NZ):
        for j in range(NX):
            outs[dz][j] = turned[(z + dz) % NZ * NX + (x + j) % NX]


def split_head(me, features, halo):
    f, g, _ = features.shape
    return pl.pallas_call(
        head_kernel,
        grid_spec=pltpu.PrefetchScalarGridSpec(
            num_scalar_prefetch=1,
            grid=(1,),
            in_specs=[full((f, g, halo))],
            out_specs=[full((NX, f, halo))] * NZ,
            scratch_shapes=[pltpu.VMEM((g, f, halo), BF)],
        ),
        out_shape=[jax.ShapeDtypeStruct((NX, f, halo), BF)] * NZ,
        compiler_params=VM,
        name="split_head",
    )(me, features)


def tail_kernel(x_ref, o_ref):
    o_ref[...] = jnp.swapaxes(x_ref[...], 0, 1)


def split_tail(features, halo):
    f, g, n = features.shape
    return pl.pallas_call(
        tail_kernel,
        grid=(n // halo - 1,),
        in_specs=[pl.BlockSpec((f, g, halo), lambda i: (0, 0, i + 1))],
        out_specs=pl.BlockSpec((g, f, halo), lambda i: (0, 0, i)),
        out_shape=hbm((g, f, n - halo), BF),
        compiler_params=VM,
        name="split_tail",
    )(features)


def regroup_kernel(*refs):
    ins, outs = refs[:NZ], refs[NZ:]
    f = ins[0].shape[1]
    for j in range(NX):
        for dz in range(NZ):
            outs[j][dz * f : (dz + 1) * f, :] = ins[dz][j]


def regroup(parts):
    _, f, halo = parts[0].shape
    return pl.pallas_call(
        regroup_kernel,
        grid=(1,),
        in_specs=[full((NX, f, halo))] * NZ,
        out_specs=[full((NZ * f, halo))] * NX,
        out_shape=[jax.ShapeDtypeStruct((NZ * f, halo), BF)] * NX,
        compiler_params=VM,
        name="regroup",
    )(*parts)


def halo_kernel(me_ref, a, b, c, d, ws_ref, wn_ref, self_ref, h_ref, w_ref):
    z, x = place(me_ref)
    rows, hid = a.shape[0], ws_ref.shape[1]
    f = rows // NZ
    total = None
    for j, part in enumerate((a, b, c, d)):
        for dz in range(NZ):
            src = ((z + (NZ - dz)) % NZ * NX + (x + (NX - j)) % NX) * f
            src = pl.multiple_of(src, f)
            w_ref[dz * f : (dz + 1) * f, :hid] = ws_ref[pl.ds(src, f), :]
            w_ref[dz * f : (dz + 1) * f, hid:] = wn_ref[pl.ds(src, f), :]
        one = lax.dot_general(
            part[...], w_ref[...], (((0,), (0,)), ((), ())), preferred_element_type=F32
        )
        total = one if total is None else total + one
    self_ref[...] = total[:, :hid]
    h = total[:, hid:]
    high = h.astype(BF)
    h_ref[:, :hid] = high
    h_ref[:, hid:] = (h - high.astype(F32)).astype(BF)


def halo_hidden(me, parts, w_self, w_neigh):
    rows, halo = parts[0].shape
    total, hid = w_self.shape
    return pl.pallas_call(
        halo_kernel,
        grid_spec=pltpu.PrefetchScalarGridSpec(
            num_scalar_prefetch=1,
            grid=(1,),
            in_specs=[full((rows, halo))] * NX + [full((total, hid))] * 2,
            out_specs=[full((halo, hid)), full((halo, 2 * hid))],
            scratch_shapes=[pltpu.VMEM((rows, 2 * hid), BF)],
        ),
        out_shape=[
            hbm((halo, hid), F32),
            jax.ShapeDtypeStruct((halo, 2 * hid), BF),
        ],
        compiler_params=VM,
        name="halo_hidden",
    )(me, *parts, w_self, w_neigh)


def mask_kernel(mask_ref, al_ref, ar_ref, head_ref, tail_ref, remote_ref, scale_ref):
    row = pl.program_id(0)
    local, halo = al_ref.shape[1] // TILE, head_ref.shape[1]
    degree = jnp.zeros((TILE, TILE), F32)
    for t in range(local + ar_ref.shape[1] // TILE):
        flag = mask_ref[row, t].astype(F32)
        if t < local:
            at = t * TILE
            tile = al_ref[:, at : at + TILE].astype(F32) * flag
            if at < halo:
                head_ref[:, at : at + TILE] = tile.astype(BF)
            else:
                tail_ref[:, at - halo : at - halo + TILE] = tile.astype(BF)
        else:
            at = (t - local) * TILE
            tile = ar_ref[:, at : at + TILE].astype(F32) * flag
            remote_ref[:, at : at + TILE] = tile.astype(BF)
        degree = degree + tile
    whole = jnp.sum(degree, axis=1, keepdims=True)
    scale_ref[...] = jnp.broadcast_to(1.0 / jnp.sqrt(whole), (TILE, TILE))


def mask_tiles(tile_mask, adj_local, adj_remote, halo):
    rows, n = adj_local.shape
    r = adj_remote.shape[1]
    line = lambda w: pl.BlockSpec((TILE, w), lambda i, _: (i, 0))
    return pl.pallas_call(
        mask_kernel,
        grid_spec=pltpu.PrefetchScalarGridSpec(
            num_scalar_prefetch=1,
            grid=(rows // TILE,),
            in_specs=[line(n), line(r)],
            out_specs=[line(halo), line(n - halo), line(r), line(TILE)],
        ),
        out_shape=[
            hbm((rows, halo), BF),
            hbm((rows, n - halo), BF),
            hbm((rows, r), BF),
            hbm((rows, TILE), F32),
        ],
        compiler_params=VM,
        name="mask_tiles",
    )(tile_mask, in_hbm(adj_local), in_hbm(adj_remote))


def near_kernel(head_ref, remote_ref, a, b, c, d, o_ref):
    halo = a.shape[0]
    total = jnp.dot(head_ref[...], a[...], preferred_element_type=F32)
    for dy, part in ((1, b), (2, c), (3, d)):
        at = (2 * dy - 1) * halo
        total = total + jnp.dot(
            remote_ref[:, at : at + halo], part[...], preferred_element_type=F32
        )
    hid = o_ref.shape[1]
    o_ref[...] = total[:, :hid] + total[:, hid:]


def far_kernel(me_ref, acc_ref, remote_ref, a, b, c, d, o_ref):
    core = me_ref[0] % 2
    halo, hid = a.shape[0], o_ref.shape[1]
    total = None
    for dy, part in enumerate((a, b, c, d)):
        at = pl.multiple_of(((2 * dy + 2 * core + 7) % NB - 1) * halo, halo)
        one = jnp.dot(remote_ref[:, pl.ds(at, halo)], part[...], preferred_element_type=F32)
        total = one if total is None else total + one
    o_ref[...] = acc_ref[...] + total[:, :hid] + total[:, hid:]


def gather_halo(kernel, scalars, arrays, parts, out):
    rows = arrays[0].shape[0]
    hid = parts[0].shape[1] // 2
    block = 256
    line = lambda w: pl.BlockSpec((block, w), lambda i, *_: (i, 0))
    return pl.pallas_call(
        kernel,
        grid_spec=pltpu.PrefetchScalarGridSpec(
            num_scalar_prefetch=len(scalars),
            grid=(rows // block,),
            in_specs=[line(a.shape[1]) for a in arrays] + [full(p.shape) for p in parts],
            out_specs=line(hid),
        ),
        out_shape=out((rows, hid), F32),
        compiler_params=VM,
    )(*scalars, *arrays, *parts)


def last_kernel(x_ref, ws_ref, wn_ref, tail_hbm, acc_hbm, scale_hbm, sh_hbm, bias_ref, o_ref,
                h_ref, s_ref, tail_ref, acc_ref, scale_ref, sem):
    halo, hid = sh_hbm.shape
    copies = [
        pltpu.make_async_copy(sh_hbm, s_ref.at[:halo], sem.at[0]),
        pltpu.make_async_copy(tail_hbm, tail_ref, sem.at[1]),
        pltpu.make_async_copy(acc_hbm, acc_ref, sem.at[2]),
        pltpu.make_async_copy(scale_hbm, scale_ref, sem.at[3]),
    ]
    for copy in copies:
        copy.start()
    first = (((0,), (0,)), ((), ()))
    h = lax.dot_general(x_ref[...], wn_ref[...], first, preferred_element_type=F32)
    high = h.astype(BF)
    h_ref[:, :hid] = high
    h_ref[:, hid:] = (h - high.astype(F32)).astype(BF)
    s_ref[halo:, :] = lax.dot_general(x_ref[...], ws_ref[...], first, preferred_element_type=F32)
    for copy in copies:
        copy.wait()
    rows, block = o_ref.shape[0], 256
    for i in range(0, rows, block):
        at = slice(i, i + block)
        both = jnp.dot(tail_ref[at, :], h_ref[...], preferred_element_type=F32)
        summed = acc_ref[at, :] + both[:, :hid] + both[:, hid:]
        scale = jnp.concatenate([scale_ref[at, :]] * (hid // TILE), axis=1)
        o_ref[at, :] = jnp.maximum(s_ref[at, :] + summed * scale + bias_ref[...], 0.0).astype(BF)


def last_step(x, w_self, w_neigh, tail, acc, scale, self_head, bias):
    rows, hid = acc.shape
    away = pl.BlockSpec(memory_space=pltpu.HBM)
    return pl.pallas_call(
        last_kernel,
        grid=(1,),
        in_specs=[full(x.shape), full(w_self.shape), full(w_neigh.shape), away, away, away, away, full(bias.shape)],
        out_specs=full((rows, hid)),
        scratch_shapes=[
            pltpu.VMEM((x.shape[1], 2 * hid), BF),
            pltpu.VMEM((rows, hid), F32),
            pltpu.VMEM(tail.shape, BF),
            pltpu.VMEM(acc.shape, F32),
            pltpu.VMEM(scale.shape, F32),
            pltpu.SemaphoreType.DMA((4,)),
        ],
        out_shape=jax.ShapeDtypeStruct((rows, hid), BF),
        compiler_params=VM,
        name="last_step",
    )(x, w_self, w_neigh, in_hbm(tail), in_hbm(acc), in_hbm(scale), in_hbm(self_head), bias)


def shards(features, adj_local, adj_remote, tile_mask, w_self, w_neigh, out_bias):
    halo = adj_remote.shape[1] // (lax.axis_size("blk") - 1)
    me = lax.axis_index(("feat", "blk")).reshape(1)
    features = in_hbm(features)

    head = split_head(me, features, halo)
    landed = [head[0]]
    for dz in range(1, NZ):
        landed.append(lax.ppermute(head[dz], "feat", feat_shift(dz, 0)))
    rest = split_tail(features, halo)
    rest = lax.all_to_all(rest, "feat", split_axis=0, concat_axis=0, tiled=True)
    rest = rest.reshape(-1, rest.shape[-1])

    live_head, live_tail, live_remote, scale = mask_tiles(tile_mask, adj_local, adj_remote, halo)
    rows = regroup(landed)
    parts = [rows[0]]
    for j in range(1, NX):
        parts.append(lax.ppermute(rows[j], "feat", feat_shift(0, j)))
    self_head, h_head = halo_hidden(me, parts, w_self, w_neigh)
    same = [h_head] + [lax.ppermute(h_head, "blk", blk_shift(dy, 0)) for dy in (1, 2, 3)]
    other = [lax.ppermute(h, "blk", blk_shift(0, 1)) for h in same]
    acc = gather_halo(near_kernel, (), (live_head, live_remote), same, jax.ShapeDtypeStruct)
    acc = gather_halo(far_kernel, (me,), (acc, live_remote), other, hbm)
    return last_step(
        rest, w_self, w_neigh, live_tail, acc, scale, self_head, out_bias[None, :]
    )


def solution(mesh):
    placed = (
        P("feat", None, "blk"),
        P(("feat", "blk"), None),
        P(("feat", "blk"), None),
        P(("feat", "blk"), None),
        P(),
        P(),
        P(),
    )

    return jax.shard_map(
        shards, mesh=mesh, in_specs=placed, out_specs=P(("feat", "blk"), None), check_vma=False
    )
```

```python
import jax
import jax.numpy as jnp
from jax import lax
from jax.experimental import pallas as pl
from jax.experimental.pallas import tpu as pltpu
from jax.sharding import PartitionSpec as P

TILE = 128
NZ = 8
NX = 4
NB = 8
EARLY = 512
BF = jnp.bfloat16
F32 = jnp.float32


VM = pltpu.CompilerParams(vmem_limit_bytes=16 << 20)


def full(shape):
    return pl.BlockSpec(shape, lambda *_: (0,) * len(shape))


def feat_shift(dz, dx):
    return [
        (z * NX + x, (z + dz) % NZ * NX + (x + dx) % NX) for z in range(NZ) for x in range(NX)
    ]


def blk_shift(dy, dc):
    return [(y * 2 + c, (y + dy) % 4 * 2 + (c + dc) % 2) for y in range(4) for c in range(2)]


def place(me_ref):
    feat = me_ref[0] // NB
    return feat // NX, feat % NX


def in_hbm(x):
    return pltpu.with_memory_space_constraint(x, pltpu.HBM)


def hbm(shape, dtype):
    return pltpu.HBM(shape, dtype)


def swap_matrix():
    r = lax.broadcasted_iota(jnp.int32, (256, 256), 0)
    c = lax.broadcasted_iota(jnp.int32, (256, 256), 1)
    hit = ((r & 15) == (c >> 4)) & ((r >> 4) == (c & 15))
    return jnp.where(hit, 1.0, 0.0).astype(BF)


def swapped(swap, block):
    n = block.shape[-1]
    out = jnp.dot(swap, block.reshape(256, n), preferred_element_type=F32)
    return out.astype(BF).reshape(16, 16, n)


def head_kernel(me_ref, x_ref, *rest):
    outs, turned = rest[:-1], rest[-1]
    swap = swap_matrix()
    f, g, _ = x_ref.shape
    for f0 in range(0, f, 16):
        for g0 in range(0, g, 16):
            turned[g0 : g0 + 16, f0 : f0 + 16, :] = swapped(swap, x_ref[f0 : f0 + 16, g0 : g0 + 16, :])
    z, x = place(me_ref)
    for dz in range(NZ):
        for j in range(NX):
            outs[dz][j] = turned[(z + dz) % NZ * NX + (x + j) % NX]


def split_head(me, features, halo):
    f, g, _ = features.shape
    return pl.pallas_call(
        head_kernel,
        grid_spec=pltpu.PrefetchScalarGridSpec(
            num_scalar_prefetch=1,
            grid=(1,),
            in_specs=[full((f, g, halo))],
            out_specs=[full((NX, f, halo))] * NZ,
            scratch_shapes=[pltpu.VMEM((g, f, halo), BF)],
        ),
        out_shape=[jax.ShapeDtypeStruct((NX, f, halo), BF)] * NZ,
        compiler_params=VM,
        name="split_head",
    )(me, features)


def tail_kernel(x_hbm, o_hbm, x_ref, o_ref, sem):
    f, g, n = x_ref.shape
    halo = x_hbm.shape[2] - n
    chunks = range(0, f, 16)
    ins = [
        pltpu.make_async_copy(
            x_hbm.at[pl.ds(f0, 16), :, pl.ds(halo, n)], x_ref.at[pl.ds(f0, 16)], sem.at[0, i]
        )
        for i, f0 in enumerate(chunks)
    ]
    for copy in ins:
        copy.start()
    swap = swap_matrix()
    outs = []
    for i, f0 in enumerate(chunks):
        ins[i].wait()
        for g0 in range(0, g, 16):
            o_ref[g0 : g0 + 16, f0 : f0 + 16, :] = swapped(swap, x_ref[f0 : f0 + 16, g0 : g0 + 16, :])
        copy = pltpu.make_async_copy(
            o_ref.at[:, pl.ds(f0, 16), :], o_hbm.at[:, pl.ds(f0, 16), :], sem.at[1, i]
        )
        copy.start()
        outs.append(copy)
    for copy in outs:
        copy.wait()


def split_tail(features, halo):
    f, g, n = features.shape
    return pl.pallas_call(
        tail_kernel,
        in_specs=[pl.BlockSpec(memory_space=pltpu.HBM)],
        out_specs=pl.BlockSpec(memory_space=pltpu.HBM),
        out_shape=hbm((g, f, n - halo), BF),
        scratch_shapes=[
            pltpu.VMEM((f, g, n - halo), BF),
            pltpu.VMEM((g, f, n - halo), BF),
            pltpu.SemaphoreType.DMA((2, f // 16)),
        ],
        compiler_params=VM,
        name="split_tail",
    )(features)


def regroup_kernel(*refs):
    ins, outs = refs[:NZ], refs[NZ:]
    f, halo = ins[0].shape[1], outs[0].shape[1]
    for j in range(NX):
        for dz in range(NZ):
            at = slice(dz * f, (dz + 1) * f)
            outs[j][at, :] = ins[dz][j, :, :halo]
            outs[NX + j][at, :] = ins[dz][j, :, halo:]


def regroup(parts, halo):
    _, f, early = parts[0].shape
    shapes = [(NZ * f, halo)] * NX + [(NZ * f, early - halo)] * NX
    return pl.pallas_call(
        regroup_kernel,
        grid=(1,),
        in_specs=[full((NX, f, early))] * NZ,
        out_specs=[full(shape) for shape in shapes],
        out_shape=[jax.ShapeDtypeStruct(shape, BF) for shape in shapes],
        compiler_params=VM,
        name="regroup",
    )(*parts)


def weights_kernel(me_ref, ws_hbm, wn_hbm, rot_ref, turned_ref, ws_ref, wn_ref, sem):
    copies = [
        pltpu.make_async_copy(ws_hbm, ws_ref, sem.at[0]),
        pltpu.make_async_copy(wn_hbm, wn_ref, sem.at[1]),
    ]
    for copy in copies:
        copy.start()
    z, x = place(me_ref)
    total, hid = ws_ref.shape
    f = total // (NZ * NX)
    for half, w_ref in enumerate((ws_ref, wn_ref)):
        copies[half].wait()
        at = slice(half * hid, (half + 1) * hid)
        turned_ref[at, :] = w_ref[...].T
        for j in range(NX):
            for dz in range(NZ):
                src = ((z + (NZ - dz)) % NZ * NX + (x + (NX - j)) % NX) * f
                to = (j * NZ + dz) * f
                rot_ref[to : to + f, at] = w_ref[pl.ds(pl.multiple_of(src, f), f), :]


def weights(me, w_self, w_neigh):
    f, hid = w_self.shape
    away = pl.BlockSpec(memory_space=pltpu.HBM)
    return pl.pallas_call(
        weights_kernel,
        grid_spec=pltpu.PrefetchScalarGridSpec(
            num_scalar_prefetch=1,
            grid=(1,),
            in_specs=[away, away],
            out_specs=[full((f, 2 * hid)), full((2 * hid, f))],
            scratch_shapes=[
                pltpu.VMEM((f, hid), BF),
                pltpu.VMEM((f, hid), BF),
                pltpu.SemaphoreType.DMA((2,)),
            ],
        ),
        out_shape=[
            jax.ShapeDtypeStruct((f, 2 * hid), BF),
            jax.ShapeDtypeStruct((2 * hid, f), BF),
        ],
        compiler_params=VM,
        name="weights",
    )(me, in_hbm(w_self), in_hbm(w_neigh))


def project(parts, rot_ref, columns):
    rows = parts[0].shape[0]
    total = None
    for j, part in enumerate(parts):
        one = lax.dot_general(
            part[...],
            rot_ref[j * rows : (j + 1) * rows, columns],
            (((0,), (0,)), ((), ())),
            preferred_element_type=F32,
        )
        total = one if total is None else total + one
    return total


def halo_kernel(a, b, c, d, rot_ref, h_ref):
    hid = h_ref.shape[1]
    h_ref[...] = project((a, b, c, d), rot_ref, slice(hid, None)).astype(BF)


def halo_hidden(parts, rot):
    rows, halo = parts[0].shape
    hid = rot.shape[1] // 2
    return pl.pallas_call(
        halo_kernel,
        grid=(1,),
        in_specs=[full((rows, halo))] * NX + [full(rot.shape)],
        out_specs=full((halo, hid)),
        out_shape=jax.ShapeDtypeStruct((halo, hid), BF),
        compiler_params=VM,
        name="halo_hidden",
    )(*parts, rot)


def mid_kernel(*refs):
    heads, mids, (rot_ref, mid_ref, acc_ref, self_ref, o_ref) = refs[:NX], refs[NX : 2 * NX], refs[2 * NX :]
    halo, hid = heads[0].shape[1], o_ref.shape[1]
    h = project(mids, rot_ref, slice(hid, None)).astype(BF)
    o_ref[...] = acc_ref[...] + jnp.dot(mid_ref[...], h, preferred_element_type=F32)
    self_ref[:halo, :] = project(heads, rot_ref, slice(0, hid))
    self_ref[halo:, :] = project(mids, rot_ref, slice(0, hid))


def mid_hidden(heads, mids, rot, live_mid, acc):
    early = heads[0].shape[1] + mids[0].shape[1]
    hid = rot.shape[1] // 2
    args = (*heads, *mids, rot, live_mid, acc)
    return pl.pallas_call(
        mid_kernel,
        grid=(1,),
        in_specs=[full(a.shape) for a in args],
        out_specs=[full((early, hid)), full(acc.shape)],
        out_shape=[hbm((early, hid), F32), jax.ShapeDtypeStruct(acc.shape, F32)],
        compiler_params=VM,
        name="mid_hidden",
    )(*args)


def mask_kernel(me_ref, mask_ref, al_hbm, ar_hbm, head_ref, mid_ref, tail_hbm, near_ref, far_ref, scale_hbm,
                al_ref, ar_ref, tail_ref, scale_ref, sem):
    block = 2 * TILE
    count = al_ref.shape[0] // block
    ins, outs = [], []
    for i in range(count):
        at = pl.ds(i * block, block)
        ins.append(
            (
                pltpu.make_async_copy(al_hbm.at[at], al_ref.at[at], sem.at[0, i]),
                pltpu.make_async_copy(ar_hbm.at[at], ar_ref.at[at], sem.at[1, i]),
            )
        )
        for copy in ins[-1]:
            copy.start()
    local, halo, mid = al_ref.shape[1] // TILE, head_ref.shape[1], mid_ref.shape[1]
    core = me_ref[0] % 2
    for i in range(count):
        for copy in ins[i]:
            copy.wait()
        for row in range(i * 2, i * 2 + 2):
            rows = slice(row * TILE, (row + 1) * TILE)
            degree = jnp.zeros((TILE, TILE), F32)
            for t in range(local + ar_ref.shape[1] // TILE):
                flag = mask_ref[row, t].astype(F32)
                at = t * TILE if t < local else (t - local) * TILE
                tile = (al_ref if t < local else ar_ref)[rows, at : at + TILE].astype(F32) * flag
                if t >= local:
                    back, inside = at // halo + 1, at % halo
                    if back % 2 == 0:
                        to, at = near_ref, (back // 2 - 1) * halo + inside
                    else:
                        slot = ((back + 1) // 2 + 4 - core) % 4
                        to, at = far_ref, pl.multiple_of(slot * halo + inside, TILE)
                elif at < halo:
                    to = head_ref
                elif at < halo + mid:
                    to, at = mid_ref, at - halo
                else:
                    to, at = tail_ref, at - halo - mid
                to[rows, pl.ds(at, TILE)] = tile.astype(BF)
                degree = degree + tile
            whole = jnp.sum(degree, axis=1, keepdims=True)
            scale_ref[rows, :] = jnp.broadcast_to(1.0 / jnp.sqrt(whole), (TILE, TILE))
        at = pl.ds(i * block, block)
        outs += [
            pltpu.make_async_copy(tail_ref.at[at], tail_hbm.at[at], sem.at[2, i]),
            pltpu.make_async_copy(scale_ref.at[at], scale_hbm.at[at], sem.at[3, i]),
        ]
        outs[-2].start()
        outs[-1].start()
    for copy in outs:
        copy.wait()


def mask_tiles(me, tile_mask, adj_local, adj_remote, halo, early):
    rows, n = adj_local.shape
    r = adj_remote.shape[1]
    away = pl.BlockSpec(memory_space=pltpu.HBM)
    return pl.pallas_call(
        mask_kernel,
        grid_spec=pltpu.PrefetchScalarGridSpec(
            num_scalar_prefetch=2,
            grid=(1,),
            in_specs=[away, away],
            out_specs=[
                full((rows, halo)),
                full((rows, early - halo)),
                away,
                full((rows, 3 * halo)),
                full((rows, 4 * halo)),
                away,
            ],
            scratch_shapes=[
                pltpu.VMEM((rows, n), BF),
                pltpu.VMEM((rows, r), BF),
                pltpu.VMEM((rows, n - early), BF),
                pltpu.VMEM((rows, TILE), F32),
                pltpu.SemaphoreType.DMA((4, rows // (2 * TILE))),
            ],
        ),
        out_shape=[
            jax.ShapeDtypeStruct((rows, halo), BF),
            jax.ShapeDtypeStruct((rows, early - halo), BF),
            hbm((rows, n - early), BF),
            jax.ShapeDtypeStruct((rows, 3 * halo), BF),
            jax.ShapeDtypeStruct((rows, 4 * halo), BF),
            hbm((rows, TILE), F32),
        ],
        compiler_params=pltpu.CompilerParams(vmem_limit_bytes=24 << 20),
        name="mask_tiles",
    )(me, tile_mask, in_hbm(adj_local), in_hbm(adj_remote))


def near_kernel(head_ref, near_ref, a, b, c, d, o_ref):
    halo = a.shape[0]
    total = jnp.dot(head_ref[...], a[...], preferred_element_type=F32)
    for i, part in enumerate((b, c, d)):
        at = slice(i * halo, (i + 1) * halo)
        total = total + jnp.dot(near_ref[:, at], part[...], preferred_element_type=F32)
    o_ref[...] = total


def far_kernel(acc_ref, far_ref, a, b, c, d, o_ref):
    halo = a.shape[0]
    total = acc_ref[...]
    for i, part in enumerate((a, b, c, d)):
        at = slice(i * halo, (i + 1) * halo)
        total = total + jnp.dot(far_ref[:, at], part[...], preferred_element_type=F32)
    o_ref[...] = total


def gather_halo(kernel, arrays, parts, out):
    rows = arrays[0].shape[0]
    hid = parts[0].shape[1]
    block = 256
    line = lambda w: pl.BlockSpec((block, w), lambda i: (i, 0))
    return pl.pallas_call(
        kernel,
        grid=(rows // block,),
        in_specs=[line(a.shape[1]) for a in arrays] + [full(p.shape) for p in parts],
        out_specs=line(hid),
        out_shape=out((rows, hid), F32),
        compiler_params=VM,
    )(*arrays, *parts)


def last_kernel(x_ref, wt_ref, tail_hbm, acc_hbm, scale_hbm, self_hbm, bias_ref, o_hbm,
                s_ref, tail_ref, acc_ref, scale_ref, o_ref, sem):
    rows, hid = acc_ref.shape
    early, block = self_hbm.shape[0], 256
    ins = []
    for i in range(rows // block):
        at = pl.ds(i * block, block)
        some = [
            pltpu.make_async_copy(tail_hbm.at[at], tail_ref.at[at], sem.at[0, i]),
            pltpu.make_async_copy(acc_hbm.at[at], acc_ref.at[at], sem.at[1, i]),
            pltpu.make_async_copy(scale_hbm.at[at], scale_ref.at[at], sem.at[2, i]),
        ]
        if i == 0:
            some.append(pltpu.make_async_copy(self_hbm, s_ref.at[pl.ds(0, early)], sem.at[3, 0]))
        for copy in some:
            copy.start()
        ins.append(some)
    ht = jnp.dot(wt_ref[hid:, :], x_ref[...], preferred_element_type=F32).astype(BF)
    s_ref[early:, :] = jnp.dot(wt_ref[:hid, :], x_ref[...], preferred_element_type=F32).T
    last = (((1,), (1,)), ((), ()))
    outs = []
    for i in range(rows // block):
        for copy in ins[i]:
            copy.wait()
        at = slice(i * block, (i + 1) * block)
        more = lax.dot_general(tail_ref[at, :], ht, last, preferred_element_type=F32)
        scale = jnp.concatenate([scale_ref[at, :]] * (hid // TILE), axis=1)
        o_ref[at, :] = jnp.maximum(
            s_ref[at, :] + (acc_ref[at, :] + more) * scale + bias_ref[...], 0.0
        ).astype(BF)
        at = pl.ds(i * block, block)
        outs.append(pltpu.make_async_copy(o_ref.at[at], o_hbm.at[at], sem.at[4, i]))
        outs[-1].start()
    for copy in outs:
        copy.wait()


def last_step(x, turned, tail, acc, scale, self_early, bias):
    rows, hid = acc.shape
    away = pl.BlockSpec(memory_space=pltpu.HBM)
    return pl.pallas_call(
        last_kernel,
        grid=(1,),
        in_specs=[full(x.shape), full(turned.shape)] + [away] * 4 + [full(bias.shape)],
        out_specs=away,
        scratch_shapes=[
            pltpu.VMEM((rows, hid), F32),
            pltpu.VMEM(tail.shape, BF),
            pltpu.VMEM(acc.shape, F32),
            pltpu.VMEM(scale.shape, F32),
            pltpu.VMEM((rows, hid), BF),
            pltpu.SemaphoreType.DMA((5, rows // 256)),
        ],
        out_shape=jax.ShapeDtypeStruct((rows, hid), BF),
        compiler_params=VM,
        name="last_step",
    )(x, turned, *(in_hbm(a) for a in (tail, acc, scale, self_early)), bias)


def shards(features, adj_local, adj_remote, tile_mask, w_self, w_neigh, out_bias):
    halo = adj_remote.shape[1] // (lax.axis_size("blk") - 1)
    me = lax.axis_index(("feat", "blk")).reshape(1)
    features = in_hbm(features)

    head = split_head(me, features, EARLY)
    landed = [head[0]]
    for dz in range(1, NZ):
        landed.append(lax.ppermute(head[dz], "feat", feat_shift(dz, 0)))
    rest = split_tail(features, EARLY)
    rest = lax.all_to_all(rest, "feat", split_axis=0, concat_axis=0, tiled=True)
    rest = rest.reshape(-1, rest.shape[-1])

    rot, turned = weights(me, w_self, w_neigh)
    live_head, live_mid, live_tail, live_near, live_far, scale = mask_tiles(
        me, tile_mask, adj_local, adj_remote, halo, EARLY
    )
    rows = regroup(landed, halo)
    parts, mids = [rows[0]], [rows[NX]]
    for j in range(1, NX):
        parts.append(lax.ppermute(rows[j], "feat", feat_shift(0, j)))
        mids.append(lax.ppermute(rows[NX + j], "feat", feat_shift(0, j)))
    h_head = halo_hidden(parts, rot)
    same = [h_head]
    for dy in (1, 2, 3):
        same.append(lax.ppermute(h_head, "blk", blk_shift(dy, 0)))
    other = [lax.ppermute(h, "blk", blk_shift(0, 1)) for h in same]
    acc = gather_halo(near_kernel, (live_head, live_near), same, jax.ShapeDtypeStruct)
    self_early, acc = mid_hidden(parts, mids, rot, live_mid, acc)
    acc = gather_halo(far_kernel, (acc, live_far), other, hbm)
    return last_step(rest, turned, live_tail, acc, scale, self_early, out_bias[None, :])


def solution(mesh):
    placed = (
        P("feat", None, "blk"),
        P(("feat", "blk"), None),
        P(("feat", "blk"), None),
        P(("feat", "blk"), None),
        P(),
        P(),
        P(),
    )

    return jax.shard_map(
        shards, mesh=mesh, in_specs=placed, out_specs=P(("feat", "blk"), None), check_vma=False
    )
```

```python
import jax
import jax.numpy as jnp
from jax import lax
from jax.experimental import pallas as pl
from jax.experimental.pallas import tpu as pltpu
from jax.sharding import PartitionSpec as P

TILE = 128
NZ = 8
NX = 4
NB = 8
EARLY = 384
BF = jnp.bfloat16
F32 = jnp.float32


VM = pltpu.CompilerParams(vmem_limit_bytes=16 << 20)


def full(shape):
    return pl.BlockSpec(shape, lambda *_: (0,) * len(shape))


def feat_shift(dz, dx):
    return [
        (z * NX + x, (z + dz) % NZ * NX + (x + dx) % NX) for z in range(NZ) for x in range(NX)
    ]


def blk_shift(dy, dc):
    return [(y * 2 + c, (y + dy) % 4 * 2 + (c + dc) % 2) for y in range(4) for c in range(2)]


def place(me_ref):
    feat = me_ref[0] // NB
    return feat // NX, feat % NX


def in_hbm(x):
    return pltpu.with_memory_space_constraint(x, pltpu.HBM)


def hbm(shape, dtype):
    return pltpu.HBM(shape, dtype)


def swap_matrix(g, z, x):
    rows = 8 * g
    r = lax.broadcasted_iota(jnp.int32, (rows, rows), 0)
    c = lax.broadcasted_iota(jnp.int32, (rows, rows), 1)
    slot = r // 8
    place_of = (slot // NX + z) % NZ * NX + (slot % NX + x) % NX
    return jnp.where(c == (r % 8) * g + place_of, 1.0, 0.0).astype(BF)


def swapped(swap, x_ref, f0, at):
    g, n = x_ref.shape[1], at.stop - at.start
    halves = [
        jnp.dot(swap, x_ref[f : f + 8, :, at].reshape(8 * g, n), preferred_element_type=F32)
        .reshape(g, 8, n)
        for f in (f0, f0 + 8)
    ]
    return jnp.concatenate(halves, axis=1).astype(BF)


def split_kernel(me_ref, x_hbm, *rest):
    heads, (tail_hbm, x_ref, tail_ref, sem) = rest[:NZ], rest[NZ:]
    f, g, n = x_ref.shape
    early = heads[0].shape[2]
    chunks = range(0, f, 16)

    def load(i, f0, start, size, which):
        at = (pl.ds(f0, 16), slice(None), pl.ds(start, size))
        return pltpu.make_async_copy(x_hbm.at[at], x_ref.at[at], sem.at[which, i])

    late = [load(i, f0, early, n - early, 0) for i, f0 in enumerate(chunks)]
    soon = [load(i, f0, 0, early, 1) for i, f0 in enumerate(chunks)]
    for copy in late + soon:
        copy.start()
    zero = jnp.int32(0)
    plain = swap_matrix(g, zero, zero)
    turned = swap_matrix(g, *place(me_ref))
    outs = []
    for i, f0 in enumerate(chunks):
        late[i].wait()
        for n0 in range(early, n, 2 * TILE):
            at = slice(n0, min(n0 + 2 * TILE, n))
            to = slice(at.start - early, at.stop - early)
            tail_ref[:, f0 : f0 + 16, to] = swapped(plain, x_ref, f0, at)
        at = (slice(None), pl.ds(f0, 16), slice(None))
        outs.append(pltpu.make_async_copy(tail_ref.at[at], tail_hbm.at[at], sem.at[2, i]))
        outs[-1].start()
    for i, f0 in enumerate(chunks):
        soon[i].wait()
        for n0 in range(0, early, 2 * TILE):
            at = slice(n0, min(n0 + 2 * TILE, early))
            block = swapped(turned, x_ref, f0, at)
            for dz in range(NZ):
                heads[dz][:, f0 : f0 + 16, at] = block[dz * NX : (dz + 1) * NX]
    for copy in outs:
        copy.wait()


def split(me, features, early):
    f, g, n = features.shape
    away = pl.BlockSpec(memory_space=pltpu.HBM)
    *heads, tail = pl.pallas_call(
        split_kernel,
        grid_spec=pltpu.PrefetchScalarGridSpec(
            num_scalar_prefetch=1,
            grid=(1,),
            in_specs=[away],
            out_specs=[full((NX, f, early))] * NZ + [away],
            scratch_shapes=[
                pltpu.VMEM((f, g, n), BF),
                pltpu.VMEM((g, f, n - early), BF),
                pltpu.SemaphoreType.DMA((3, f // 16)),
            ],
        ),
        out_shape=[jax.ShapeDtypeStruct((NX, f, early), BF)] * NZ + [hbm((g, f, n - early), BF)],
        compiler_params=VM,
        name="split",
    )(me, features)
    return heads, tail


def regroup_kernel(*refs):
    ins, outs = refs[:NZ], refs[NZ:]
    f, halo = ins[0].shape[1], outs[0].shape[1]
    for j in range(NX):
        for dz in range(NZ):
            at = slice(dz * f, (dz + 1) * f)
            outs[j][at, :] = ins[dz][j, :, :halo]
            outs[NX + j][at, :] = ins[dz][j, :, halo:]


def regroup(parts, halo):
    _, f, early = parts[0].shape
    shapes = [(NZ * f, halo)] * NX + [(NZ * f, early - halo)] * NX
    return pl.pallas_call(
        regroup_kernel,
        grid=(1,),
        in_specs=[full((NX, f, early))] * NZ,
        out_specs=[full(shape) for shape in shapes],
        out_shape=[jax.ShapeDtypeStruct(shape, BF) for shape in shapes],
        compiler_params=VM,
        name="regroup",
    )(*parts)


def weights_kernel(me_ref, ws_hbm, wn_hbm, rot_ref, turned_ref, ws_ref, wn_ref, sem):
    copies = [
        pltpu.make_async_copy(ws_hbm, ws_ref, sem.at[0]),
        pltpu.make_async_copy(wn_hbm, wn_ref, sem.at[1]),
    ]
    for copy in copies:
        copy.start()
    z, x = place(me_ref)
    total, hid = ws_ref.shape
    f = total // (NZ * NX)
    for half, w_ref in enumerate((ws_ref, wn_ref)):
        copies[half].wait()
        at = slice(half * hid, (half + 1) * hid)
        turned_ref[at, :] = w_ref[...].T
        for j in range(NX):
            for dz in range(NZ):
                src = ((z + (NZ - dz)) % NZ * NX + (x + (NX - j)) % NX) * f
                to = (j * NZ + dz) * f
                rot_ref[to : to + f, at] = w_ref[pl.ds(pl.multiple_of(src, f), f), :]


def weights(me, w_self, w_neigh):
    f, hid = w_self.shape
    away = pl.BlockSpec(memory_space=pltpu.HBM)
    return pl.pallas_call(
        weights_kernel,
        grid_spec=pltpu.PrefetchScalarGridSpec(
            num_scalar_prefetch=1,
            grid=(1,),
            in_specs=[away, away],
            out_specs=[full((f, 2 * hid)), full((2 * hid, f))],
            scratch_shapes=[
                pltpu.VMEM((f, hid), BF),
                pltpu.VMEM((f, hid), BF),
                pltpu.SemaphoreType.DMA((2,)),
            ],
        ),
        out_shape=[
            jax.ShapeDtypeStruct((f, 2 * hid), BF),
            jax.ShapeDtypeStruct((2 * hid, f), BF),
        ],
        compiler_params=VM,
        name="weights",
    )(me, in_hbm(w_self), in_hbm(w_neigh))


def halo_kernel(a, b, c, d, rot_ref, h_ref):
    rows, (halo, hid) = a.shape[0], h_ref.shape
    total = None
    for j, part in enumerate((a, b, c, d)):
        one = lax.dot_general(
            part[...],
            rot_ref[j * rows : (j + 1) * rows, hid:],
            (((0,), (0,)), ((), ())),
            preferred_element_type=F32,
        )
        total = one if total is None else total + one
    h_ref[...] = total.astype(BF)


def halo_hidden(parts, rot, halo):
    hid = rot.shape[1] // 2
    return pl.pallas_call(
        halo_kernel,
        grid=(1,),
        in_specs=[full(parts[0].shape)] * NX + [full(rot.shape)],
        out_specs=full((halo, hid)),
        out_shape=jax.ShapeDtypeStruct((halo, hid), BF),
        compiler_params=VM,
        name="halo_hidden",
    )(*parts, rot)


def mid_kernel(*refs):
    halves, (rot_ref, own_ref, head_ref, mid_ref, self_ref, o_ref) = refs[: 2 * NX], refs[2 * NX :]
    halo, hid = own_ref.shape
    rows = halves[0].shape[0]
    total = [None, None]
    for k, part in enumerate(halves):
        j, which = k % NX, k // NX
        one = lax.dot_general(
            part[...],
            rot_ref[j * rows : (j + 1) * rows, : hid * (1 + which)],
            (((0,), (0,)), ((), ())),
            preferred_element_type=F32,
        )
        total[which] = one if j == 0 else total[which] + one
    self_ref[:halo, :] = total[0]
    self_ref[halo:, :] = total[1][:, :hid]
    h = total[1][:, hid:].astype(BF)
    o_ref[...] = jnp.dot(head_ref[...], own_ref[...], preferred_element_type=F32) + jnp.dot(
        mid_ref[...], h, preferred_element_type=F32
    )


def mid_hidden(parts, mids, rot, own, live_head, live_mid):
    early, rows, hid = parts[0].shape[1] + mids[0].shape[1], live_mid.shape[0], own.shape[1]
    args = (*parts, *mids, rot, own, live_head, live_mid)
    return pl.pallas_call(
        mid_kernel,
        grid=(1,),
        in_specs=[full(a.shape) for a in args],
        out_specs=[full((early, hid)), full((rows, hid))],
        out_shape=[hbm((early, hid), F32), jax.ShapeDtypeStruct((rows, hid), F32)],
        compiler_params=VM,
        name="mid_hidden",
    )(*args)


def mask_kernel(me_ref, mask_ref, al_hbm, ar_hbm, head_ref, mid_ref, tail_hbm, near_ref, far_ref, scale_hbm,
                al_ref, ar_ref, tail_ref, scale_ref, sem):
    block = 2 * TILE
    count = al_ref.shape[0] // block
    ins, outs = [], []
    for i in range(count):
        at = pl.ds(i * block, block)
        ins.append(
            (
                pltpu.make_async_copy(al_hbm.at[at], al_ref.at[at], sem.at[0, i]),
                pltpu.make_async_copy(ar_hbm.at[at], ar_ref.at[at], sem.at[1, i]),
            )
        )
        for copy in ins[-1]:
            copy.start()
    local, halo, mid = al_ref.shape[1] // TILE, head_ref.shape[1], mid_ref.shape[1]
    core = me_ref[0] % 2
    for i in range(count):
        for copy in ins[i]:
            copy.wait()
        for row in range(i * 2, i * 2 + 2):
            rows = slice(row * TILE, (row + 1) * TILE)
            degree = jnp.zeros((TILE, TILE), F32)
            for t in range(local + ar_ref.shape[1] // TILE):
                flag = mask_ref[row, t].astype(F32)
                at = t * TILE if t < local else (t - local) * TILE
                tile = (al_ref if t < local else ar_ref)[rows, at : at + TILE].astype(F32) * flag
                if t >= local:
                    back, inside = at // halo + 1, at % halo
                    if back % 2 == 0:
                        to, at = near_ref, (back // 2 - 1) * halo + inside
                    else:
                        slot = ((back + 1) // 2 + 4 - core) % 4
                        to, at = far_ref, pl.multiple_of(slot * halo + inside, TILE)
                elif at < halo:
                    to = head_ref
                elif at < halo + mid:
                    to, at = mid_ref, at - halo
                else:
                    to, at = tail_ref, at - halo - mid
                to[rows, pl.ds(at, TILE)] = tile.astype(BF)
                degree = degree + tile
            whole = jnp.sum(degree, axis=1, keepdims=True)
            scale_ref[rows, :] = jnp.broadcast_to(1.0 / jnp.sqrt(whole), (TILE, TILE))
        at = pl.ds(i * block, block)
        outs += [
            pltpu.make_async_copy(tail_ref.at[at], tail_hbm.at[at], sem.at[2, i]),
            pltpu.make_async_copy(scale_ref.at[at], scale_hbm.at[at], sem.at[3, i]),
        ]
        outs[-2].start()
        outs[-1].start()
    for copy in outs:
        copy.wait()


def mask_tiles(me, tile_mask, adj_local, adj_remote, halo, early):
    rows, n = adj_local.shape
    r = adj_remote.shape[1]
    away = pl.BlockSpec(memory_space=pltpu.HBM)
    return pl.pallas_call(
        mask_kernel,
        grid_spec=pltpu.PrefetchScalarGridSpec(
            num_scalar_prefetch=2,
            grid=(1,),
            in_specs=[away, away],
            out_specs=[
                full((rows, halo)),
                full((rows, early - halo)),
                away,
                full((rows, 3 * halo)),
                full((rows, 4 * halo)),
                away,
            ],
            scratch_shapes=[
                pltpu.VMEM((rows, n), BF),
                pltpu.VMEM((rows, r), BF),
                pltpu.VMEM((rows, n - early), BF),
                pltpu.VMEM((rows, TILE), F32),
                pltpu.SemaphoreType.DMA((4, rows // (2 * TILE))),
            ],
        ),
        out_shape=[
            jax.ShapeDtypeStruct((rows, halo), BF),
            jax.ShapeDtypeStruct((rows, early - halo), BF),
            hbm((rows, n - early), BF),
            jax.ShapeDtypeStruct((rows, 3 * halo), BF),
            jax.ShapeDtypeStruct((rows, 4 * halo), BF),
            hbm((rows, TILE), F32),
        ],
        compiler_params=pltpu.CompilerParams(vmem_limit_bytes=24 << 20),
        name="mask_tiles",
    )(me, tile_mask, in_hbm(adj_local), in_hbm(adj_remote))


def gather_kernel(acc_ref, live_ref, *rest):
    parts, o_ref = rest[:-1], rest[-1]
    halo = parts[0].shape[0]
    total = acc_ref[...]
    for i, part in enumerate(parts):
        at = slice(i * halo, (i + 1) * halo)
        total = total + jnp.dot(live_ref[:, at], part[...], preferred_element_type=F32)
    o_ref[...] = total


def gather_halo(arrays, parts):
    rows = arrays[0].shape[0]
    hid = parts[0].shape[1]
    block = 256
    line = lambda w: pl.BlockSpec((block, w), lambda i: (i, 0))
    return pl.pallas_call(
        gather_kernel,
        grid=(rows // block,),
        in_specs=[line(a.shape[1]) for a in arrays] + [full(p.shape) for p in parts],
        out_specs=line(hid),
        out_shape=jax.ShapeDtypeStruct((rows, hid), F32),
        compiler_params=VM,
    )(*arrays, *parts)


def last_kernel(x_ref, wt_ref, acc_ref, tail_hbm, scale_hbm, self_hbm, bias_ref, o_hbm,
                s_ref, tail_ref, scale_ref, o_ref, sem):
    rows, hid = acc_ref.shape
    early, block = self_hbm.shape[0], 256
    ins = []
    for i in range(rows // block):
        at = pl.ds(i * block, block)
        some = [
            pltpu.make_async_copy(tail_hbm.at[at], tail_ref.at[at], sem.at[0, i]),
            pltpu.make_async_copy(scale_hbm.at[at], scale_ref.at[at], sem.at[2, i]),
        ]
        if i == 0:
            some.append(pltpu.make_async_copy(self_hbm, s_ref.at[pl.ds(0, early)], sem.at[3, 0]))
        for copy in some:
            copy.start()
        ins.append(some)
    ht = jnp.dot(wt_ref[hid:, :], x_ref[...], preferred_element_type=F32).astype(BF)
    s_ref[early:, :] = jnp.dot(wt_ref[:hid, :], x_ref[...], preferred_element_type=F32).T
    last = (((1,), (1,)), ((), ()))
    outs = []
    for i in range(rows // block):
        for copy in ins[i]:
            copy.wait()
        at = slice(i * block, (i + 1) * block)
        more = lax.dot_general(tail_ref[at, :], ht, last, preferred_element_type=F32)
        scale = jnp.concatenate([scale_ref[at, :]] * (hid // TILE), axis=1)
        o_ref[at, :] = jnp.maximum(
            s_ref[at, :] + (acc_ref[at, :] + more) * scale + bias_ref[...], 0.0
        ).astype(BF)
        at = pl.ds(i * block, block)
        outs.append(pltpu.make_async_copy(o_ref.at[at], o_hbm.at[at], sem.at[4, i]))
        outs[-1].start()
    for copy in outs:
        copy.wait()


def last_step(x, turned, acc, tail, scale, self_early, bias):
    rows, hid = acc.shape
    away = pl.BlockSpec(memory_space=pltpu.HBM)
    return pl.pallas_call(
        last_kernel,
        grid=(1,),
        in_specs=[full(x.shape), full(turned.shape), full(acc.shape)] + [away] * 3 + [full(bias.shape)],
        out_specs=away,
        scratch_shapes=[
            pltpu.VMEM((rows, hid), F32),
            pltpu.VMEM(tail.shape, BF),
            pltpu.VMEM(scale.shape, F32),
            pltpu.VMEM((rows, hid), BF),
            pltpu.SemaphoreType.DMA((5, rows // 256)),
        ],
        out_shape=jax.ShapeDtypeStruct((rows, hid), BF),
        compiler_params=VM,
        name="last_step",
    )(x, turned, acc, *(in_hbm(a) for a in (tail, scale, self_early)), bias)


def shards(features, adj_local, adj_remote, tile_mask, w_self, w_neigh, out_bias):
    halo = adj_remote.shape[1] // (lax.axis_size("blk") - 1)
    me = lax.axis_index(("feat", "blk")).reshape(1)
    features = in_hbm(features)

    head, rest = split(me, features, EARLY)
    landed = [head[0]]
    for dz in range(1, NZ):
        landed.append(lax.ppermute(head[dz], "feat", feat_shift(dz, 0)))
    rest = lax.all_to_all(rest, "feat", split_axis=0, concat_axis=0, tiled=True)
    rest = rest.reshape(-1, rest.shape[-1])

    rot, turned = weights(me, w_self, w_neigh)
    live_head, live_mid, live_tail, live_near, live_far, scale = mask_tiles(
        me, tile_mask, adj_local, adj_remote, halo, EARLY
    )
    rows = regroup(landed, halo)
    parts, mids = [rows[0]], [rows[NX]]
    for j in range(1, NX):
        parts.append(lax.ppermute(rows[j], "feat", feat_shift(0, j)))
        mids.append(lax.ppermute(rows[NX + j], "feat", feat_shift(0, j)))
    h_head = halo_hidden(parts, rot, halo)
    same = []
    for dy in (1, 2, 3):
        same.append(lax.ppermute(h_head, "blk", blk_shift(dy, 0)))
    other = [lax.ppermute(h, "blk", blk_shift(0, 1)) for h in [h_head] + same]
    self_early, acc = mid_hidden(parts, mids, rot, h_head, live_head, live_mid)
    acc = gather_halo((acc, live_near), same)
    acc = gather_halo((acc, live_far), other)
    return last_step(rest, turned, acc, live_tail, scale, self_early, out_bias[None, :])


def solution(mesh):
    placed = (
        P("feat", None, "blk"),
        P(("feat", "blk"), None),
        P(("feat", "blk"), None),
        P(("feat", "blk"), None),
        P(),
        P(),
        P(),
    )

    return jax.shard_map(
        shards, mesh=mesh, in_specs=placed, out_specs=P(("feat", "blk"), None), check_vma=False
    )
```

```python
import jax
import jax.numpy as jnp
from jax import lax
from jax.experimental import pallas as pl
from jax.experimental.pallas import tpu as pltpu
from jax.sharding import PartitionSpec as P

TILE = 128
NZ = 8
NX = 4
NB = 8
EARLY = 384
BF = jnp.bfloat16
F32 = jnp.float32


VM = pltpu.CompilerParams(vmem_limit_bytes=16 << 20)


def full(shape):
    return pl.BlockSpec(shape, lambda *_: (0,) * len(shape))


def feat_shift(dz, dx):
    return [
        (z * NX + x, (z + dz) % NZ * NX + (x + dx) % NX) for z in range(NZ) for x in range(NX)
    ]


def blk_shift(dy, dc):
    return [(y * 2 + c, (y + dy) % 4 * 2 + (c + dc) % 2) for y in range(4) for c in range(2)]


def place(me_ref):
    feat = me_ref[0] // NB
    return feat // NX, feat % NX


def in_hbm(x):
    return pltpu.with_memory_space_constraint(x, pltpu.HBM)


def hbm(shape, dtype):
    return pltpu.HBM(shape, dtype)


def swap_matrix(g, z, x):
    rows = 8 * g
    r = lax.broadcasted_iota(jnp.int32, (rows, rows), 0)
    c = lax.broadcasted_iota(jnp.int32, (rows, rows), 1)
    place_of = (((r >> 5) + z) & (NZ - 1)) * NX + (((r >> 3) + x) & (NX - 1))
    return jnp.where(c == (r & 7) * g + place_of, 1.0, 0.0).astype(BF)


def swapped(swap, x_ref, f0, at):
    g, n = x_ref.shape[1], at.stop - at.start
    halves = [
        jnp.dot(swap, x_ref[f : f + 8, :, at].reshape(8 * g, n), preferred_element_type=F32)
        .reshape(g, 8, n)
        for f in (f0, f0 + 8)
    ]
    return jnp.concatenate(halves, axis=1).astype(BF)


def split_kernel(me_ref, x_hbm, *rest):
    heads, (tail_hbm, x_ref, tail_ref, sem) = rest[:NZ], rest[NZ:]
    f, g, n = x_ref.shape
    early = heads[0].shape[2]
    chunks = range(0, f, 16)

    def load(i, f0, start, size, which):
        at = (pl.ds(f0, 16), slice(None), pl.ds(start, size))
        return pltpu.make_async_copy(x_hbm.at[at], x_ref.at[at], sem.at[which, i])

    late = [load(i, f0, early, n - early, 0) for i, f0 in enumerate(chunks)]
    soon = [load(i, f0, 0, early, 1) for i, f0 in enumerate(chunks)]
    for copy in late + soon:
        copy.start()
    zero = jnp.int32(0)
    plain = swap_matrix(g, zero, zero)
    turned = swap_matrix(g, *place(me_ref))
    outs = []
    for i, f0 in enumerate(chunks):
        late[i].wait()
        for n0 in range(early, n, 2 * TILE):
            at = slice(n0, min(n0 + 2 * TILE, n))
            to = slice(at.start - early, at.stop - early)
            tail_ref[:, f0 : f0 + 16, to] = swapped(plain, x_ref, f0, at)
        at = (slice(None), pl.ds(f0, 16), slice(None))
        outs.append(pltpu.make_async_copy(tail_ref.at[at], tail_hbm.at[at], sem.at[2, i]))
        outs[-1].start()
    for i, f0 in enumerate(chunks):
        soon[i].wait()
        for n0 in range(0, early, 2 * TILE):
            at = slice(n0, min(n0 + 2 * TILE, early))
            block = swapped(turned, x_ref, f0, at)
            for dz in range(NZ):
                heads[dz][:, f0 : f0 + 16, at] = block[dz * NX : (dz + 1) * NX]
    for copy in outs:
        copy.wait()


def split(me, features, early):
    f, g, n = features.shape
    away = pl.BlockSpec(memory_space=pltpu.HBM)
    *heads, tail = pl.pallas_call(
        split_kernel,
        grid_spec=pltpu.PrefetchScalarGridSpec(
            num_scalar_prefetch=1,
            grid=(1,),
            in_specs=[away],
            out_specs=[full((NX, f, early))] * NZ + [away],
            scratch_shapes=[
                pltpu.VMEM((f, g, n), BF),
                pltpu.VMEM((g, f, n - early), BF),
                pltpu.SemaphoreType.DMA((3, f // 16)),
            ],
        ),
        out_shape=[jax.ShapeDtypeStruct((NX, f, early), BF)] * NZ + [hbm((g, f, n - early), BF)],
        compiler_params=VM,
        name="split",
    )(me, features)
    return heads, tail


def regroup_kernel(*refs):
    ins, outs = refs[:NZ], refs[NZ:]
    f, halo = ins[0].shape[1], outs[0].shape[1]
    for j in range(NX):
        for dz in range(NZ):
            at = slice(dz * f, (dz + 1) * f)
            outs[j][at, :] = ins[dz][j, :, :halo]
            outs[NX + j][at, :] = ins[dz][j, :, halo:]


def regroup(parts, halo):
    _, f, early = parts[0].shape
    shapes = [(NZ * f, halo)] * NX + [(NZ * f, early - halo)] * NX
    return pl.pallas_call(
        regroup_kernel,
        grid=(1,),
        in_specs=[full((NX, f, early))] * NZ,
        out_specs=[full(shape) for shape in shapes],
        out_shape=[jax.ShapeDtypeStruct(shape, BF) for shape in shapes],
        compiler_params=VM,
        name="regroup",
    )(*parts)


def weights_kernel(me_ref, ws_hbm, wn_hbm, rot_ref, turned_ref, ws_ref, wn_ref, sem):
    copies = [
        pltpu.make_async_copy(ws_hbm, ws_ref, sem.at[0]),
        pltpu.make_async_copy(wn_hbm, wn_ref, sem.at[1]),
    ]
    for copy in copies:
        copy.start()
    z, x = place(me_ref)
    total, hid = ws_ref.shape
    f = total // (NZ * NX)
    for half, w_ref in enumerate((ws_ref, wn_ref)):
        copies[half].wait()
        at = slice(half * hid, (half + 1) * hid)
        turned_ref[:, at] = w_ref[...]
        for j in range(NX):
            for dz in range(NZ):
                src = ((z + (NZ - dz)) % NZ * NX + (x + (NX - j)) % NX) * f
                to = (j * NZ + dz) * f
                rot_ref[to : to + f, at] = w_ref[pl.ds(pl.multiple_of(src, f), f), :]


def weights(me, w_self, w_neigh):
    f, hid = w_self.shape
    away = pl.BlockSpec(memory_space=pltpu.HBM)
    return pl.pallas_call(
        weights_kernel,
        grid_spec=pltpu.PrefetchScalarGridSpec(
            num_scalar_prefetch=1,
            grid=(1,),
            in_specs=[away, away],
            out_specs=[full((f, 2 * hid))] * 2,
            scratch_shapes=[
                pltpu.VMEM((f, hid), BF),
                pltpu.VMEM((f, hid), BF),
                pltpu.SemaphoreType.DMA((2,)),
            ],
        ),
        out_shape=[
            jax.ShapeDtypeStruct((f, 2 * hid), BF),
            jax.ShapeDtypeStruct((f, 2 * hid), BF),
        ],
        compiler_params=VM,
        name="weights",
    )(me, in_hbm(w_self), in_hbm(w_neigh))


def halo_kernel(a, b, c, d, rot_ref, h_ref):
    rows, (halo, hid) = a.shape[0], h_ref.shape
    total = None
    for j, part in enumerate((a, b, c, d)):
        one = lax.dot_general(
            part[...],
            rot_ref[j * rows : (j + 1) * rows, hid:],
            (((0,), (0,)), ((), ())),
            preferred_element_type=F32,
        )
        total = one if total is None else total + one
    h_ref[...] = total.astype(BF)


def halo_hidden(parts, rot, halo):
    hid = rot.shape[1] // 2
    return pl.pallas_call(
        halo_kernel,
        grid=(1,),
        in_specs=[full(parts[0].shape)] * NX + [full(rot.shape)],
        out_specs=full((halo, hid)),
        out_shape=jax.ShapeDtypeStruct((halo, hid), BF),
        compiler_params=VM,
        name="halo_hidden",
    )(*parts, rot)


def mid_kernel(*refs):
    halves, (rot_ref, own_ref, head_ref, mid_ref, self_ref, o_ref) = refs[: 2 * NX], refs[2 * NX :]
    halo, hid = own_ref.shape
    rows = halves[0].shape[0]
    total = [None, None]
    for k, part in enumerate(halves):
        j, which = k % NX, k // NX
        one = lax.dot_general(
            part[...],
            rot_ref[j * rows : (j + 1) * rows, : hid * (1 + which)],
            (((0,), (0,)), ((), ())),
            preferred_element_type=F32,
        )
        total[which] = one if j == 0 else total[which] + one
    self_ref[:halo, :] = total[0]
    self_ref[halo:, :] = total[1][:, :hid]
    h = total[1][:, hid:].astype(BF)
    o_ref[...] = jnp.dot(head_ref[...], own_ref[...], preferred_element_type=F32) + jnp.dot(
        mid_ref[...], h, preferred_element_type=F32
    )


def mid_hidden(parts, mids, rot, own, live_head, live_mid):
    early, rows, hid = parts[0].shape[1] + mids[0].shape[1], live_mid.shape[0], own.shape[1]
    args = (*parts, *mids, rot, own, live_head, live_mid)
    return pl.pallas_call(
        mid_kernel,
        grid=(1,),
        in_specs=[full(a.shape) for a in args],
        out_specs=[full((early, hid)), full((rows, hid))],
        out_shape=[hbm((early, hid), F32), jax.ShapeDtypeStruct((rows, hid), F32)],
        compiler_params=VM,
        name="mid_hidden",
    )(*args)


def mask_kernel(me_ref, mask_ref, al_hbm, ar_hbm, head_ref, mid_ref, tail_hbm, near_ref, far_ref, scale_hbm,
                al_ref, ar_ref, tail_ref, scale_ref, sem):
    block = 2 * TILE
    count = al_ref.shape[0] // block
    ins, outs = [], []
    for i in range(count):
        at = pl.ds(i * block, block)
        ins.append(
            (
                pltpu.make_async_copy(al_hbm.at[at], al_ref.at[at], sem.at[0, i]),
                pltpu.make_async_copy(ar_hbm.at[at], ar_ref.at[at], sem.at[1, i]),
            )
        )
        for copy in ins[-1]:
            copy.start()
    local, halo, mid = al_ref.shape[1] // TILE, head_ref.shape[1], mid_ref.shape[1]
    core = me_ref[0] % 2
    for i in range(count):
        for copy in ins[i]:
            copy.wait()
        for row in range(i * 2, i * 2 + 2):
            rows = slice(row * TILE, (row + 1) * TILE)
            degree = jnp.zeros((TILE, TILE), F32)
            for t in range(local + ar_ref.shape[1] // TILE):
                flag = jnp.full((TILE, TILE), mask_ref[row, t].astype(F32)).astype(BF)
                at = t * TILE if t < local else (t - local) * TILE
                tile = (al_ref if t < local else ar_ref)[rows, at : at + TILE] * flag
                if t >= local:
                    back, inside = at // halo + 1, at % halo
                    if back % 2 == 0:
                        to, at = near_ref, (back // 2 - 1) * halo + inside
                    else:
                        slot = ((back + 1) // 2 + 4 - core) % 4
                        to, at = far_ref, pl.multiple_of(slot * halo + inside, TILE)
                elif at < halo:
                    to = head_ref
                elif at < halo + mid:
                    to, at = mid_ref, at - halo
                else:
                    to, at = tail_ref, at - halo - mid
                to[rows, pl.ds(at, TILE)] = tile
                degree = degree + tile.astype(F32)
            whole = jnp.sum(degree, axis=1, keepdims=True)
            scale_ref[rows, :] = jnp.broadcast_to(1.0 / jnp.sqrt(whole), (TILE, TILE))
        at = pl.ds(i * block, block)
        outs += [
            pltpu.make_async_copy(tail_ref.at[at], tail_hbm.at[at], sem.at[2, i]),
            pltpu.make_async_copy(scale_ref.at[at], scale_hbm.at[at], sem.at[3, i]),
        ]
        outs[-2].start()
        outs[-1].start()
    for copy in outs:
        copy.wait()


def mask_tiles(me, tile_mask, adj_local, adj_remote, halo, early):
    rows, n = adj_local.shape
    r = adj_remote.shape[1]
    away = pl.BlockSpec(memory_space=pltpu.HBM)
    return pl.pallas_call(
        mask_kernel,
        grid_spec=pltpu.PrefetchScalarGridSpec(
            num_scalar_prefetch=2,
            grid=(1,),
            in_specs=[away, away],
            out_specs=[
                full((rows, halo)),
                full((rows, early - halo)),
                away,
                full((rows, 3 * halo)),
                full((rows, 4 * halo)),
                away,
            ],
            scratch_shapes=[
                pltpu.VMEM((rows, n), BF),
                pltpu.VMEM((rows, r), BF),
                pltpu.VMEM((rows, n - early), BF),
                pltpu.VMEM((rows, TILE), F32),
                pltpu.SemaphoreType.DMA((4, rows // (2 * TILE))),
            ],
        ),
        out_shape=[
            jax.ShapeDtypeStruct((rows, halo), BF),
            jax.ShapeDtypeStruct((rows, early - halo), BF),
            hbm((rows, n - early), BF),
            jax.ShapeDtypeStruct((rows, 3 * halo), BF),
            jax.ShapeDtypeStruct((rows, 4 * halo), BF),
            hbm((rows, TILE), F32),
        ],
        compiler_params=pltpu.CompilerParams(vmem_limit_bytes=24 << 20),
        name="mask_tiles",
    )(me, tile_mask, in_hbm(adj_local), in_hbm(adj_remote))


def gather_kernel(acc_ref, live_ref, *rest):
    parts, o_ref = rest[:-1], rest[-1]
    halo = parts[0].shape[0]
    total = acc_ref[...]
    for i, part in enumerate(parts):
        at = slice(i * halo, (i + 1) * halo)
        total = total + jnp.dot(live_ref[:, at], part[...], preferred_element_type=F32)
    o_ref[...] = total


def gather_halo(arrays, parts):
    rows = arrays[0].shape[0]
    hid = parts[0].shape[1]
    block = 256
    line = lambda w: pl.BlockSpec((block, w), lambda i: (i, 0))
    return pl.pallas_call(
        gather_kernel,
        grid=(rows // block,),
        in_specs=[line(a.shape[1]) for a in arrays] + [full(p.shape) for p in parts],
        out_specs=line(hid),
        out_shape=jax.ShapeDtypeStruct((rows, hid), F32),
        compiler_params=VM,
    )(*arrays, *parts)


def last_kernel(x_ref, w_ref, acc_ref, tail_hbm, scale_hbm, self_hbm, bias_ref, o_hbm,
                s_ref, h_ref, tail_ref, scale_ref, o_ref, sem):
    rows, hid = acc_ref.shape
    early, block = self_hbm.shape[0], 256
    ins = []
    for i in range(rows // block):
        at = pl.ds(i * block, block)
        some = [
            pltpu.make_async_copy(tail_hbm.at[at], tail_ref.at[at], sem.at[0, i]),
            pltpu.make_async_copy(scale_hbm.at[at], scale_ref.at[at], sem.at[2, i]),
        ]
        if i == 0:
            some.append(pltpu.make_async_copy(self_hbm, s_ref.at[pl.ds(0, early)], sem.at[3, 0]))
        for copy in some:
            copy.start()
        ins.append(some)
    first = (((0,), (0,)), ((), ()))
    for n0 in range(0, x_ref.shape[1], x_ref.shape[1]):
        at = slice(n0, n0 + x_ref.shape[1])
        both = lax.dot_general(x_ref[:, at], w_ref[...], first, preferred_element_type=F32)
        s_ref[pl.ds(early + at.start, at.stop - at.start), :] = both[:, :hid]
        h_ref[at, :] = both[:, hid:].astype(BF)
    outs = []
    for i in range(rows // block):
        for copy in ins[i]:
            copy.wait()
        at = slice(i * block, (i + 1) * block)
        more = jnp.dot(tail_ref[at, :], h_ref[...], preferred_element_type=F32)
        scale = jnp.concatenate([scale_ref[at, :]] * (hid // TILE), axis=1)
        o_ref[at, :] = jnp.maximum(
            s_ref[at, :] + (acc_ref[at, :] + more) * scale + bias_ref[...], 0.0
        ).astype(BF)
        at = pl.ds(i * block, block)
        outs.append(pltpu.make_async_copy(o_ref.at[at], o_hbm.at[at], sem.at[4, i]))
        outs[-1].start()
    for copy in outs:
        copy.wait()


def last_step(x, turned, acc, tail, scale, self_early, bias):
    rows, hid = acc.shape
    away = pl.BlockSpec(memory_space=pltpu.HBM)
    return pl.pallas_call(
        last_kernel,
        grid=(1,),
        in_specs=[full(x.shape), full(turned.shape), full(acc.shape)] + [away] * 3 + [full(bias.shape)],
        out_specs=away,
        scratch_shapes=[
            pltpu.VMEM((rows, hid), F32),
            pltpu.VMEM((x.shape[1], hid), BF),
            pltpu.VMEM(tail.shape, BF),
            pltpu.VMEM(scale.shape, F32),
            pltpu.VMEM((rows, hid), BF),
            pltpu.SemaphoreType.DMA((5, rows // 256)),
        ],
        out_shape=jax.ShapeDtypeStruct((rows, hid), BF),
        compiler_params=VM,
        name="last_step",
    )(x, turned, acc, *(in_hbm(a) for a in (tail, scale, self_early)), bias)


def shards(features, adj_local, adj_remote, tile_mask, w_self, w_neigh, out_bias):
    halo = adj_remote.shape[1] // (lax.axis_size("blk") - 1)
    me = lax.axis_index(("feat", "blk")).reshape(1)
    features = in_hbm(features)

    head, rest = split(me, features, EARLY)
    landed = [head[0]]
    for dz in range(1, NZ):
        landed.append(lax.ppermute(head[dz], "feat", feat_shift(dz, 0)))
    rest = lax.all_to_all(rest, "feat", split_axis=0, concat_axis=0, tiled=True)
    rest = rest.reshape(-1, rest.shape[-1])

    rot, turned = weights(me, w_self, w_neigh)
    live_head, live_mid, live_tail, live_near, live_far, scale = mask_tiles(
        me, tile_mask, adj_local, adj_remote, halo, EARLY
    )
    rows = regroup(landed, halo)
    parts, mids = [rows[0]], [rows[NX]]
    for j in range(1, NX):
        parts.append(lax.ppermute(rows[j], "feat", feat_shift(0, j)))
        mids.append(lax.ppermute(rows[NX + j], "feat", feat_shift(0, j)))
    h_head = halo_hidden(parts, rot, halo)
    same = []
    for dy in (1, 2, 3):
        same.append(lax.ppermute(h_head, "blk", blk_shift(dy, 0)))
    other = [lax.ppermute(h, "blk", blk_shift(0, 1)) for h in [h_head] + same]
    self_early, acc = mid_hidden(parts, mids, rot, h_head, live_head, live_mid)
    acc = gather_halo((acc, live_near), same)
    acc = gather_halo((acc, live_far), other)
    return last_step(rest, turned, acc, live_tail, scale, self_early, out_bias[None, :])


def solution(mesh):
    placed = (
        P("feat", None, "blk"),
        P(("feat", "blk"), None),
        P(("feat", "blk"), None),
        P(("feat", "blk"), None),
        P(),
        P(),
        P(),
    )

    return jax.shard_map(
        shards, mesh=mesh, in_specs=placed, out_specs=P(("feat", "blk"), None), check_vma=False
    )
```

```python
import jax
import jax.numpy as jnp
from jax import lax
from jax.experimental import pallas as pl
from jax.experimental.pallas import tpu as pltpu
from jax.sharding import PartitionSpec as P

TILE = 128
NZ = 8
NX = 4
NB = 8
EARLY = 384
BF = jnp.bfloat16
F32 = jnp.float32


VM = pltpu.CompilerParams(vmem_limit_bytes=16 << 20)


def full(shape):
    return pl.BlockSpec(shape, lambda *_: (0,) * len(shape))


def feat_shift(dz, dx):
    return [
        (z * NX + x, (z + dz) % NZ * NX + (x + dx) % NX) for z in range(NZ) for x in range(NX)
    ]


def way_shift(dz):
    pairs = []
    for feat in range(NZ * NX):
        for b in range(NB):
            z = (feat // NX + (1 - 2 * (b % 2)) * dz) % NZ
            pairs.append((feat * NB + b, (z * NX + feat % NX) * NB + b))
    return pairs


def blk_shift(dy, dc):
    return [(y * 2 + c, (y + dy) % 4 * 2 + (c + dc) % 2) for y in range(4) for c in range(2)]


def place(me_ref):
    feat = me_ref[0] // NB
    return feat // NX, feat % NX


def way_of(me_ref):
    return 1 - 2 * (me_ref[0] % 2)


def in_hbm(x):
    return pltpu.with_memory_space_constraint(x, pltpu.HBM)


def hbm(shape, dtype):
    return pltpu.HBM(shape, dtype)


def swap_matrix(g, z, x, way):
    rows = 8 * g
    r = lax.broadcasted_iota(jnp.int32, (rows, rows), 0)
    c = lax.broadcasted_iota(jnp.int32, (rows, rows), 1)
    slot = r >> 5
    step = jnp.where(slot <= NZ // 2, slot, NZ // 2 - slot) * way
    place_of = ((step + z) & (NZ - 1)) * NX + (((r >> 3) + x) & (NX - 1))
    return jnp.where(c == (r & 7) * g + place_of, 1.0, 0.0).astype(BF)


def swapped(swap, x_ref, f0, at):
    g, n = x_ref.shape[1], at.stop - at.start
    halves = [
        jnp.dot(swap, x_ref[f : f + 8, :, at].reshape(8 * g, n), preferred_element_type=F32)
        .reshape(g, 8, n)
        for f in (f0, f0 + 8)
    ]
    return jnp.concatenate(halves, axis=1).astype(BF)


def split_kernel(me_ref, x_hbm, *rest):
    own_ref, keep_ref, four_ref, give_ref, tail_hbm, x_ref, tail_ref, sem = rest
    f, g, n = x_ref.shape
    early = own_ref.shape[2]
    chunks = range(0, f, 16)

    def load(i, f0, start, size, which):
        at = (pl.ds(f0, 16), slice(None), pl.ds(start, size))
        return pltpu.make_async_copy(x_hbm.at[at], x_ref.at[at], sem.at[which, i])

    late = [load(i, f0, early, n - early, 0) for i, f0 in enumerate(chunks)]
    soon = [load(i, f0, 0, early, 1) for i, f0 in enumerate(chunks)]
    for copy in late + soon:
        copy.start()
    r = lax.broadcasted_iota(jnp.int32, (8 * g, 8 * g), 0)
    c = lax.broadcasted_iota(jnp.int32, (8 * g, 8 * g), 1)
    plain = jnp.where(c == (r & 7) * g + (r >> 3), 1.0, 0.0).astype(BF)
    turned = swap_matrix(g, *place(me_ref), way_of(me_ref))
    outs = []
    for i, f0 in enumerate(chunks):
        late[i].wait()
        for n0 in range(early, n, 2 * TILE):
            at = slice(n0, min(n0 + 2 * TILE, n))
            to = slice(at.start - early, at.stop - early)
            tail_ref[:, f0 : f0 + 16, to] = swapped(plain, x_ref, f0, at)
        at = (slice(None), pl.ds(f0, 16), slice(None))
        outs.append(pltpu.make_async_copy(tail_ref.at[at], tail_hbm.at[at], sem.at[2, i]))
        outs[-1].start()
    for i, f0 in enumerate(chunks):
        soon[i].wait()
        for n0 in range(0, early, 2 * TILE):
            at = slice(n0, min(n0 + 2 * TILE, early))
            block = swapped(turned, x_ref, f0, at)
            own_ref[:, f0 : f0 + 16, at] = block[:NX]
            four_ref[:, f0 : f0 + 16, at] = block[4 * NX : 5 * NX]
            for k in range(3):
                keep_ref[k, :, f0 : f0 + 16, at] = block[(k + 1) * NX : (k + 2) * NX]
                give_ref[k, :, f0 : f0 + 16, at] = block[(k + 5) * NX : (k + 6) * NX]
    for copy in outs:
        copy.wait()


def split(me, features, early):
    f, g, n = features.shape
    away = pl.BlockSpec(memory_space=pltpu.HBM)
    one, three = (NX, f, early), (3, NX, f, early)
    return pl.pallas_call(
        split_kernel,
        grid_spec=pltpu.PrefetchScalarGridSpec(
            num_scalar_prefetch=1,
            grid=(1,),
            in_specs=[away],
            out_specs=[full(one), full(three), full(one), full(three), away],
            scratch_shapes=[
                pltpu.VMEM((f, g, n), BF),
                pltpu.VMEM((g, f, n - early), BF),
                pltpu.SemaphoreType.DMA((3, f // 16)),
            ],
        ),
        out_shape=[jax.ShapeDtypeStruct(shape, BF) for shape in (one, three, one, three)]
        + [hbm((g, f, n - early), BF)],
        compiler_params=VM,
        name="split",
    )(me, features)


def join_kernel(keep_ref, got_ref, *outs):
    for k, out in enumerate(outs):
        out[0] = keep_ref[k]
        out[1] = got_ref[k]


def join(keep, got):
    _, nx, f, early = keep.shape
    return pl.pallas_call(
        join_kernel,
        grid=(1,),
        in_specs=[full(keep.shape)] * 2,
        out_specs=[full((2, nx, f, early))] * 3,
        out_shape=[jax.ShapeDtypeStruct((2, nx, f, early), BF)] * 3,
        compiler_params=VM,
        name="join",
    )(keep, got)


def pack_kernel(a, b, c, o_ref):
    for k, part in enumerate((a, b, c)):
        o_ref[k] = part[1]


def pack(parts):
    _, nx, f, early = parts[0].shape
    return pl.pallas_call(
        pack_kernel,
        grid=(1,),
        in_specs=[full(parts[0].shape)] * 3,
        out_specs=full((3, nx, f, early)),
        out_shape=jax.ShapeDtypeStruct((3, nx, f, early), BF),
        compiler_params=VM,
        name="pack",
    )(*parts)


def regroup_kernel(own, a, b, c, four, back, *outs):
    f, halo = own.shape[1], outs[0].shape[1]
    for j in range(NX):
        pieces = [own[j], a[0, j], b[0, j], c[0, j], four[j]] + [back[k, j] for k in range(3)]
        for slot, piece in enumerate(pieces):
            at = slice(slot * f, (slot + 1) * f)
            outs[j][at, :] = piece[:, :halo]
            outs[NX + j][at, :] = piece[:, halo:]


def regroup(own, landed, four, back, halo):
    _, f, early = own.shape
    args = (own, *landed, four, back)
    shapes = [(NZ * f, halo)] * NX + [(NZ * f, early - halo)] * NX
    return pl.pallas_call(
        regroup_kernel,
        grid=(1,),
        in_specs=[full(a.shape) for a in args],
        out_specs=[full(shape) for shape in shapes],
        out_shape=[jax.ShapeDtypeStruct(shape, BF) for shape in shapes],
        compiler_params=VM,
        name="regroup",
    )(*args)


def weights_kernel(me_ref, ws_hbm, wn_hbm, rot_ref, turned_ref, ws_ref, wn_ref, sem):
    copies = [
        pltpu.make_async_copy(ws_hbm, ws_ref, sem.at[0]),
        pltpu.make_async_copy(wn_hbm, wn_ref, sem.at[1]),
    ]
    for copy in copies:
        copy.start()
    (z, x), way = place(me_ref), way_of(me_ref)
    total, hid = ws_ref.shape
    f = total // (NZ * NX)
    for half, w_ref in enumerate((ws_ref, wn_ref)):
        copies[half].wait()
        at = slice(half * hid, (half + 1) * hid)
        turned_ref[:, at] = w_ref[...]
        for j in range(NX):
            for dz in range(NZ):
                step = -dz if dz <= NZ // 2 else dz - NZ // 2
                src = (((z + way * step + NZ) % NZ) * NX + (x + (NX - j)) % NX) * f
                to = (j * NZ + dz) * f
                rot_ref[to : to + f, at] = w_ref[pl.ds(pl.multiple_of(src, f), f), :]


def weights(me, w_self, w_neigh):
    f, hid = w_self.shape
    away = pl.BlockSpec(memory_space=pltpu.HBM)
    return pl.pallas_call(
        weights_kernel,
        grid_spec=pltpu.PrefetchScalarGridSpec(
            num_scalar_prefetch=1,
            grid=(1,),
            in_specs=[away, away],
            out_specs=[full((f, 2 * hid))] * 2,
            scratch_shapes=[
                pltpu.VMEM((f, hid), BF),
                pltpu.VMEM((f, hid), BF),
                pltpu.SemaphoreType.DMA((2,)),
            ],
        ),
        out_shape=[
            jax.ShapeDtypeStruct((f, 2 * hid), BF),
            jax.ShapeDtypeStruct((f, 2 * hid), BF),
        ],
        compiler_params=VM,
        name="weights",
    )(me, in_hbm(w_self), in_hbm(w_neigh))


def halo_kernel(a, b, c, d, rot_ref, h_ref):
    rows, (halo, hid) = a.shape[0], h_ref.shape
    total = None
    for j, part in enumerate((a, b, c, d)):
        one = lax.dot_general(
            part[...],
            rot_ref[j * rows : (j + 1) * rows, hid:],
            (((0,), (0,)), ((), ())),
            preferred_element_type=F32,
        )
        total = one if total is None else total + one
    h_ref[...] = total.astype(BF)


def halo_hidden(parts, rot, halo):
    hid = rot.shape[1] // 2
    return pl.pallas_call(
        halo_kernel,
        grid=(1,),
        in_specs=[full(parts[0].shape)] * NX + [full(rot.shape)],
        out_specs=full((halo, hid)),
        out_shape=jax.ShapeDtypeStruct((halo, hid), BF),
        compiler_params=VM,
        name="halo_hidden",
    )(*parts, rot)


def mid_kernel(*refs):
    halves, (rot_ref, own_ref, head_ref, mid_ref, self_ref, o_ref) = refs[: 2 * NX], refs[2 * NX :]
    halo, hid = own_ref.shape
    rows = halves[0].shape[0]
    total = [None, None]
    for k, part in enumerate(halves):
        j, which = k % NX, k // NX
        one = lax.dot_general(
            part[...],
            rot_ref[j * rows : (j + 1) * rows, : hid * (1 + which)],
            (((0,), (0,)), ((), ())),
            preferred_element_type=F32,
        )
        total[which] = one if j == 0 else total[which] + one
    self_ref[:halo, :] = total[0]
    self_ref[halo:, :] = total[1][:, :hid]
    h = total[1][:, hid:].astype(BF)
    o_ref[...] = jnp.dot(head_ref[...], own_ref[...], preferred_element_type=F32) + jnp.dot(
        mid_ref[...], h, preferred_element_type=F32
    )


def mid_hidden(parts, mids, rot, own, live_head, live_mid):
    early, rows, hid = parts[0].shape[1] + mids[0].shape[1], live_mid.shape[0], own.shape[1]
    args = (*parts, *mids, rot, own, live_head, live_mid)
    return pl.pallas_call(
        mid_kernel,
        grid=(1,),
        in_specs=[full(a.shape) for a in args],
        out_specs=[full((early, hid)), full((rows, hid))],
        out_shape=[hbm((early, hid), F32), jax.ShapeDtypeStruct((rows, hid), F32)],
        compiler_params=VM,
        name="mid_hidden",
    )(*args)


def mask_kernel(me_ref, mask_ref, al_hbm, ar_hbm, head_ref, mid_ref, tail_hbm, near_ref, far_ref, scale_hbm,
                al_ref, ar_ref, tail_ref, scale_ref, sem):
    block = 2 * TILE
    count = al_ref.shape[0] // block
    ins, outs = [], []
    for i in range(count):
        at = pl.ds(i * block, block)
        ins.append(
            (
                pltpu.make_async_copy(al_hbm.at[at], al_ref.at[at], sem.at[0, i]),
                pltpu.make_async_copy(ar_hbm.at[at], ar_ref.at[at], sem.at[1, i]),
            )
        )
        for copy in ins[-1]:
            copy.start()
    local, halo, mid = al_ref.shape[1] // TILE, head_ref.shape[1], mid_ref.shape[1]
    core = me_ref[0] % 2
    for i in range(count):
        for copy in ins[i]:
            copy.wait()
        for row in range(i * 2, i * 2 + 2):
            rows = slice(row * TILE, (row + 1) * TILE)
            degree = jnp.zeros((TILE, TILE), F32)
            for t in range(local + ar_ref.shape[1] // TILE):
                flag = jnp.full((TILE, TILE), mask_ref[row, t].astype(F32)).astype(BF)
                at = t * TILE if t < local else (t - local) * TILE
                tile = (al_ref if t < local else ar_ref)[rows, at : at + TILE] * flag
                if t >= local:
                    back, inside = at // halo + 1, at % halo
                    if back % 2 == 0:
                        to, at = near_ref, (back // 2 - 1) * halo + inside
                    else:
                        slot = ((back + 1) // 2 + 4 - core) % 4
                        to, at = far_ref, pl.multiple_of(slot * halo + inside, TILE)
                elif at < halo:
                    to = head_ref
                elif at < halo + mid:
                    to, at = mid_ref, at - halo
                else:
                    to, at = tail_ref, at - halo - mid
                to[rows, pl.ds(at, TILE)] = tile
                degree = degree + tile.astype(F32)
            whole = jnp.sum(degree, axis=1, keepdims=True)
            scale_ref[rows, :] = jnp.broadcast_to(1.0 / jnp.sqrt(whole), (TILE, TILE))
        at = pl.ds(i * block, block)
        outs += [
            pltpu.make_async_copy(tail_ref.at[at], tail_hbm.at[at], sem.at[2, i]),
            pltpu.make_async_copy(scale_ref.at[at], scale_hbm.at[at], sem.at[3, i]),
        ]
        outs[-2].start()
        outs[-1].start()
    for copy in outs:
        copy.wait()


def mask_tiles(me, tile_mask, adj_local, adj_remote, halo, early):
    rows, n = adj_local.shape
    r = adj_remote.shape[1]
    away = pl.BlockSpec(memory_space=pltpu.HBM)
    return pl.pallas_call(
        mask_kernel,
        grid_spec=pltpu.PrefetchScalarGridSpec(
            num_scalar_prefetch=2,
            grid=(1,),
            in_specs=[away, away],
            out_specs=[
                full((rows, halo)),
                full((rows, early - halo)),
                away,
                full((rows, 3 * halo)),
                full((rows, 4 * halo)),
                away,
            ],
            scratch_shapes=[
                pltpu.VMEM((rows, n), BF),
                pltpu.VMEM((rows, r), BF),
                pltpu.VMEM((rows, n - early), BF),
                pltpu.VMEM((rows, TILE), F32),
                pltpu.SemaphoreType.DMA((4, rows // (2 * TILE))),
            ],
        ),
        out_shape=[
            jax.ShapeDtypeStruct((rows, halo), BF),
            jax.ShapeDtypeStruct((rows, early - halo), BF),
            hbm((rows, n - early), BF),
            jax.ShapeDtypeStruct((rows, 3 * halo), BF),
            jax.ShapeDtypeStruct((rows, 4 * halo), BF),
            hbm((rows, TILE), F32),
        ],
        compiler_params=pltpu.CompilerParams(vmem_limit_bytes=24 << 20),
        name="mask_tiles",
    )(me, tile_mask, in_hbm(adj_local), in_hbm(adj_remote))


def gather_kernel(acc_ref, live_ref, *rest):
    parts, o_ref = rest[:-1], rest[-1]
    halo = parts[0].shape[0]
    total = acc_ref[...]
    for i, part in enumerate(parts):
        at = slice(i * halo, (i + 1) * halo)
        total = total + jnp.dot(live_ref[:, at], part[...], preferred_element_type=F32)
    o_ref[...] = total


def gather_halo(arrays, parts):
    rows = arrays[0].shape[0]
    hid = parts[0].shape[1]
    block = 256
    line = lambda w: pl.BlockSpec((block, w), lambda i: (i, 0))
    return pl.pallas_call(
        gather_kernel,
        grid=(rows // block,),
        in_specs=[line(a.shape[1]) for a in arrays] + [full(p.shape) for p in parts],
        out_specs=line(hid),
        out_shape=jax.ShapeDtypeStruct((rows, hid), F32),
        compiler_params=VM,
    )(*arrays, *parts)


def last_kernel(x_ref, w_ref, acc_ref, tail_hbm, scale_hbm, self_hbm, bias_ref, o_hbm,
                s_ref, h_ref, tail_ref, scale_ref, o_ref, sem):
    rows, hid = acc_ref.shape
    early, block = self_hbm.shape[0], 256
    ins = []
    for i in range(rows // block):
        at = pl.ds(i * block, block)
        some = [
            pltpu.make_async_copy(tail_hbm.at[at], tail_ref.at[at], sem.at[0, i]),
            pltpu.make_async_copy(scale_hbm.at[at], scale_ref.at[at], sem.at[2, i]),
        ]
        if i == 0:
            some.append(pltpu.make_async_copy(self_hbm, s_ref.at[pl.ds(0, early)], sem.at[3, 0]))
        for copy in some:
            copy.start()
        ins.append(some)
    first = (((0,), (0,)), ((), ()))
    for n0 in range(0, x_ref.shape[1], x_ref.shape[1]):
        at = slice(n0, n0 + x_ref.shape[1])
        both = lax.dot_general(x_ref[:, at], w_ref[...], first, preferred_element_type=F32)
        s_ref[pl.ds(early + at.start, at.stop - at.start), :] = both[:, :hid]
        h_ref[at, :] = both[:, hid:].astype(BF)
    outs = []
    for i in range(rows // block):
        for copy in ins[i]:
            copy.wait()
        at = slice(i * block, (i + 1) * block)
        more = jnp.dot(tail_ref[at, :], h_ref[...], preferred_element_type=F32)
        scale = jnp.concatenate([scale_ref[at, :]] * (hid // TILE), axis=1)
        o_ref[at, :] = jnp.maximum(
            s_ref[at, :] + (acc_ref[at, :] + more) * scale + bias_ref[...], 0.0
        ).astype(BF)
        at = pl.ds(i * block, block)
        outs.append(pltpu.make_async_copy(o_ref.at[at], o_hbm.at[at], sem.at[4, i]))
        outs[-1].start()
    for copy in outs:
        copy.wait()


def last_step(x, turned, acc, tail, scale, self_early, bias):
    rows, hid = acc.shape
    away = pl.BlockSpec(memory_space=pltpu.HBM)
    return pl.pallas_call(
        last_kernel,
        grid=(1,),
        in_specs=[full(x.shape), full(turned.shape), full(acc.shape)] + [away] * 3 + [full(bias.shape)],
        out_specs=away,
        scratch_shapes=[
            pltpu.VMEM((rows, hid), F32),
            pltpu.VMEM((x.shape[1], hid), BF),
            pltpu.VMEM(tail.shape, BF),
            pltpu.VMEM(scale.shape, F32),
            pltpu.VMEM((rows, hid), BF),
            pltpu.SemaphoreType.DMA((5, rows // 256)),
        ],
        out_shape=jax.ShapeDtypeStruct((rows, hid), BF),
        compiler_params=VM,
        name="last_step",
    )(x, turned, acc, *(in_hbm(a) for a in (tail, scale, self_early)), bias)


def shards(features, adj_local, adj_remote, tile_mask, w_self, w_neigh, out_bias):
    halo = adj_remote.shape[1] // (lax.axis_size("blk") - 1)
    me = lax.axis_index(("feat", "blk")).reshape(1)
    features = in_hbm(features)

    own, keep, four, give, rest = split(me, features, EARLY)
    got = lax.ppermute(give, "blk", blk_shift(0, 1))
    four = lax.ppermute(four, "feat", feat_shift(NZ // 2, 0))
    landed = []
    for k, part in enumerate(join(keep, got)):
        landed.append(lax.ppermute(part, ("feat", "blk"), way_shift(k + 1)))
    rest = lax.all_to_all(rest, "feat", split_axis=0, concat_axis=0, tiled=True)
    rest = rest.reshape(-1, rest.shape[-1])

    rot, turned = weights(me, w_self, w_neigh)
    live_head, live_mid, live_tail, live_near, live_far, scale = mask_tiles(
        me, tile_mask, adj_local, adj_remote, halo, EARLY
    )
    back = lax.ppermute(pack(landed), "blk", blk_shift(0, 1))
    rows = regroup(own, landed, four, back, halo)
    parts, mids = [rows[0]], [rows[NX]]
    for j in range(1, NX):
        parts.append(lax.ppermute(rows[j], "feat", feat_shift(0, j)))
        mids.append(lax.ppermute(rows[NX + j], "feat", feat_shift(0, j)))
    h_head = halo_hidden(parts, rot, halo)
    same = []
    for dy in (1, 2, 3):
        same.append(lax.ppermute(h_head, "blk", blk_shift(dy, 0)))
    other = [lax.ppermute(h, "blk", blk_shift(0, 1)) for h in [h_head] + same]
    self_early, acc = mid_hidden(parts, mids, rot, h_head, live_head, live_mid)
    acc = gather_halo((acc, live_near), same)
    acc = gather_halo((acc, live_far), other)
    return last_step(rest, turned, acc, live_tail, scale, self_early, out_bias[None, :])


def solution(mesh):
    placed = (
        P("feat", None, "blk"),
        P(("feat", "blk"), None),
        P(("feat", "blk"), None),
        P(("feat", "blk"), None),
        P(),
        P(),
        P(),
    )

    return jax.shard_map(
        shards, mesh=mesh, in_specs=placed, out_specs=P(("feat", "blk"), None), check_vma=False
    )
```

```python
import jax
import jax.numpy as jnp
from jax import lax
from jax.experimental import pallas as pl
from jax.experimental.pallas import tpu as pltpu
from jax.sharding import PartitionSpec as P

TILE = 128
NZ = 8
NX = 4
NB = 8
EARLY = 384
BF = jnp.bfloat16
F32 = jnp.float32


VM = pltpu.CompilerParams(vmem_limit_bytes=16 << 20)


def full(shape):
    return pl.BlockSpec(shape, lambda *_: (0,) * len(shape))


def feat_shift(dz, dx):
    return [
        (z * NX + x, (z + dz) % NZ * NX + (x + dx) % NX) for z in range(NZ) for x in range(NX)
    ]


def blk_shift(dy, dc):
    return [(y * 2 + c, (y + dy) % 4 * 2 + (c + dc) % 2) for y in range(4) for c in range(2)]


def place(me_ref):
    feat = me_ref[0] // NB
    return feat // NX, feat % NX


def in_hbm(x):
    return pltpu.with_memory_space_constraint(x, pltpu.HBM)


def hbm(shape, dtype):
    return pltpu.HBM(shape, dtype)


def swap_matrix(g, z, x):
    rows = 8 * g
    r = lax.broadcasted_iota(jnp.int32, (rows, rows), 0)
    c = lax.broadcasted_iota(jnp.int32, (rows, rows), 1)
    place_of = (((r >> 5) + z) & (NZ - 1)) * NX + (((r >> 3) + x) & (NX - 1))
    return jnp.where(c == (r & 7) * g + place_of, 1.0, 0.0).astype(BF)


def swapped(swap, x_ref, f0, at):
    g, n = x_ref.shape[1], at.stop - at.start
    halves = [
        jnp.dot(swap, x_ref[f : f + 8, :, at].reshape(8 * g, n), preferred_element_type=F32)
        .reshape(g, 8, n)
        for f in (f0, f0 + 8)
    ]
    return jnp.concatenate(halves, axis=1).astype(BF)


def split_kernel(me_ref, x_hbm, *rest):
    heads, (tail_hbm, x_ref, tail_ref, sem) = rest[:NZ], rest[NZ:]
    f, g, n = x_ref.shape
    early = heads[0].shape[2]
    chunks = range(0, f, 16)

    def load(i, f0, start, size, which):
        at = (pl.ds(f0, 16), slice(None), pl.ds(start, size))
        return pltpu.make_async_copy(x_hbm.at[at], x_ref.at[at], sem.at[which, i])

    late = [load(i, f0, early, n - early, 0) for i, f0 in enumerate(chunks)]
    soon = [load(i, f0, 0, early, 1) for i, f0 in enumerate(chunks)]
    for copy in late + soon:
        copy.start()
    zero = jnp.int32(0)
    plain = swap_matrix(g, zero, zero)
    turned = swap_matrix(g, *place(me_ref))
    outs = []
    for i, f0 in enumerate(chunks):
        late[i].wait()
        for n0 in range(early, n, n - early):
            at = slice(n0, n)
            to = slice(at.start - early, at.stop - early)
            tail_ref[:, f0 : f0 + 16, to] = swapped(plain, x_ref, f0, at)
        at = (slice(None), pl.ds(f0, 16), slice(None))
        outs.append(pltpu.make_async_copy(tail_ref.at[at], tail_hbm.at[at], sem.at[2, i]))
        outs[-1].start()
    for i, f0 in enumerate(chunks):
        soon[i].wait()
        for n0 in range(0, early, early):
            at = slice(n0, early)
            block = swapped(turned, x_ref, f0, at)
            for dz in range(NZ):
                heads[dz][:, f0 : f0 + 16, at] = block[dz * NX : (dz + 1) * NX]
    for copy in outs:
        copy.wait()


def split(me, features, early):
    f, g, n = features.shape
    away = pl.BlockSpec(memory_space=pltpu.HBM)
    *heads, tail = pl.pallas_call(
        split_kernel,
        grid_spec=pltpu.PrefetchScalarGridSpec(
            num_scalar_prefetch=1,
            grid=(1,),
            in_specs=[away],
            out_specs=[full((NX, f, early))] * NZ + [away],
            scratch_shapes=[
                pltpu.VMEM((f, g, n), BF),
                pltpu.VMEM((g, f, n - early), BF),
                pltpu.SemaphoreType.DMA((3, f // 16)),
            ],
        ),
        out_shape=[jax.ShapeDtypeStruct((NX, f, early), BF)] * NZ + [hbm((g, f, n - early), BF)],
        compiler_params=VM,
        name="split",
    )(me, features)
    return heads, tail


def regroup_kernel(*refs):
    ins, outs = refs[:NZ], refs[NZ:]
    f, halo = ins[0].shape[1], outs[0].shape[1]
    for j in range(NX):
        for dz in range(NZ):
            at = slice(dz * f, (dz + 1) * f)
            outs[j][at, :] = ins[dz][j, :, :halo]
            outs[NX + j][at, :] = ins[dz][j, :, halo:]


def regroup(parts, halo):
    _, f, early = parts[0].shape
    shapes = [(NZ * f, halo)] * NX + [(NZ * f, early - halo)] * NX
    return pl.pallas_call(
        regroup_kernel,
        grid=(1,),
        in_specs=[full((NX, f, early))] * NZ,
        out_specs=[full(shape) for shape in shapes],
        out_shape=[jax.ShapeDtypeStruct(shape, BF) for shape in shapes],
        compiler_params=VM,
        name="regroup",
    )(*parts)


def weights_kernel(me_ref, ws_hbm, wn_hbm, rot_ref, turned_ref, ws_ref, wn_ref, sem):
    copies = [
        pltpu.make_async_copy(ws_hbm, ws_ref, sem.at[0]),
        pltpu.make_async_copy(wn_hbm, wn_ref, sem.at[1]),
    ]
    for copy in copies:
        copy.start()
    z, x = place(me_ref)
    total, hid = ws_ref.shape
    f = total // (NZ * NX)
    for half, w_ref in enumerate((ws_ref, wn_ref)):
        copies[half].wait()
        at = slice(half * hid, (half + 1) * hid)
        turned_ref[:, at] = w_ref[...]
        for j in range(NX):
            for dz in range(NZ):
                src = ((z + (NZ - dz)) % NZ * NX + (x + (NX - j)) % NX) * f
                to = (j * NZ + dz) * f
                rot_ref[to : to + f, at] = w_ref[pl.ds(pl.multiple_of(src, f), f), :]


def weights(me, w_self, w_neigh):
    f, hid = w_self.shape
    away = pl.BlockSpec(memory_space=pltpu.HBM)
    return pl.pallas_call(
        weights_kernel,
        grid_spec=pltpu.PrefetchScalarGridSpec(
            num_scalar_prefetch=1,
            grid=(1,),
            in_specs=[away, away],
            out_specs=[full((f, 2 * hid))] * 2,
            scratch_shapes=[
                pltpu.VMEM((f, hid), BF),
                pltpu.VMEM((f, hid), BF),
                pltpu.SemaphoreType.DMA((2,)),
            ],
        ),
        out_shape=[
            jax.ShapeDtypeStruct((f, 2 * hid), BF),
            jax.ShapeDtypeStruct((f, 2 * hid), BF),
        ],
        compiler_params=VM,
        name="weights",
    )(me, in_hbm(w_self), in_hbm(w_neigh))


def halo_kernel(a, b, c, d, rot_ref, h_ref):
    rows, (halo, hid) = a.shape[0], h_ref.shape
    total = None
    for j, part in enumerate((a, b, c, d)):
        one = lax.dot_general(
            part[...],
            rot_ref[j * rows : (j + 1) * rows, hid:],
            (((0,), (0,)), ((), ())),
            preferred_element_type=F32,
        )
        total = one if total is None else total + one
    h_ref[...] = total.astype(BF)


def halo_hidden(parts, rot, halo):
    hid = rot.shape[1] // 2
    return pl.pallas_call(
        halo_kernel,
        grid=(1,),
        in_specs=[full(parts[0].shape)] * NX + [full(rot.shape)],
        out_specs=full((halo, hid)),
        out_shape=jax.ShapeDtypeStruct((halo, hid), BF),
        compiler_params=VM,
        name="halo_hidden",
    )(*parts, rot)


def mid_kernel(*refs):
    halves, (rot_ref, own_ref, head_ref, mid_ref, self_ref, o_ref) = refs[: 2 * NX], refs[2 * NX :]
    halo, hid = own_ref.shape
    rows = halves[0].shape[0]
    total = [None, None]
    for k, part in enumerate(halves):
        j, which = k % NX, k // NX
        one = lax.dot_general(
            part[...],
            rot_ref[j * rows : (j + 1) * rows, : hid * (1 + which)],
            (((0,), (0,)), ((), ())),
            preferred_element_type=F32,
        )
        total[which] = one if j == 0 else total[which] + one
    self_ref[:halo, :] = total[0]
    self_ref[halo:, :] = total[1][:, :hid]
    h = total[1][:, hid:].astype(BF)
    o_ref[...] = jnp.dot(head_ref[...], own_ref[...], preferred_element_type=F32) + jnp.dot(
        mid_ref[...], h, preferred_element_type=F32
    )


def mid_hidden(parts, mids, rot, own, live_head, live_mid):
    early, rows, hid = parts[0].shape[1] + mids[0].shape[1], live_mid.shape[0], own.shape[1]
    args = (*parts, *mids, rot, own, live_head, live_mid)
    return pl.pallas_call(
        mid_kernel,
        grid=(1,),
        in_specs=[full(a.shape) for a in args],
        out_specs=[full((early, hid)), full((rows, hid))],
        out_shape=[hbm((early, hid), F32), jax.ShapeDtypeStruct((rows, hid), F32)],
        compiler_params=VM,
        name="mid_hidden",
    )(*args)


def mask_kernel(me_ref, mask_ref, al_hbm, ar_hbm, head_ref, mid_ref, tail_hbm, near_ref, far_ref, scale_hbm,
                al_ref, ar_ref, tail_ref, scale_ref, sem):
    block = 2 * TILE
    count = al_ref.shape[0] // block
    ins, outs = [], []
    for i in range(count):
        at = pl.ds(i * block, block)
        ins.append(
            (
                pltpu.make_async_copy(al_hbm.at[at], al_ref.at[at], sem.at[0, i]),
                pltpu.make_async_copy(ar_hbm.at[at], ar_ref.at[at], sem.at[1, i]),
            )
        )
        for copy in ins[-1]:
            copy.start()
    local, halo, mid = al_ref.shape[1] // TILE, head_ref.shape[1], mid_ref.shape[1]
    core = me_ref[0] % 2
    for i in range(count):
        for copy in ins[i]:
            copy.wait()
        for row in range(i * 2, i * 2 + 2):
            rows = slice(row * TILE, (row + 1) * TILE)
            degree = jnp.zeros((TILE, TILE), F32)
            for t in range(local + ar_ref.shape[1] // TILE):
                flag = jnp.full((TILE, TILE), mask_ref[row, t].astype(F32)).astype(BF)
                at = t * TILE if t < local else (t - local) * TILE
                tile = (al_ref if t < local else ar_ref)[rows, at : at + TILE] * flag
                if t >= local:
                    back, inside = at // halo + 1, at % halo
                    if back % 2 == 0:
                        to, at = near_ref, (back // 2 - 1) * halo + inside
                    else:
                        slot = ((back + 1) // 2 + 4 - core) % 4
                        to, at = far_ref, pl.multiple_of(slot * halo + inside, TILE)
                elif at < halo:
                    to = head_ref
                elif at < halo + mid:
                    to, at = mid_ref, at - halo
                else:
                    to, at = tail_ref, at - halo - mid
                to[rows, pl.ds(at, TILE)] = tile
                degree = degree + tile.astype(F32)
            whole = jnp.sum(degree, axis=1, keepdims=True)
            scale_ref[rows, :] = jnp.broadcast_to(1.0 / jnp.sqrt(whole), (TILE, TILE))
        at = pl.ds(i * block, block)
        outs += [
            pltpu.make_async_copy(tail_ref.at[at], tail_hbm.at[at], sem.at[2, i]),
            pltpu.make_async_copy(scale_ref.at[at], scale_hbm.at[at], sem.at[3, i]),
        ]
        outs[-2].start()
        outs[-1].start()
    for copy in outs:
        copy.wait()


def mask_tiles(me, tile_mask, adj_local, adj_remote, halo, early):
    rows, n = adj_local.shape
    r = adj_remote.shape[1]
    away = pl.BlockSpec(memory_space=pltpu.HBM)
    return pl.pallas_call(
        mask_kernel,
        grid_spec=pltpu.PrefetchScalarGridSpec(
            num_scalar_prefetch=2,
            grid=(1,),
            in_specs=[away, away],
            out_specs=[
                full((rows, halo)),
                full((rows, early - halo)),
                away,
                full((rows, 3 * halo)),
                full((rows, 4 * halo)),
                away,
            ],
            scratch_shapes=[
                pltpu.VMEM((rows, n), BF),
                pltpu.VMEM((rows, r), BF),
                pltpu.VMEM((rows, n - early), BF),
                pltpu.VMEM((rows, TILE), F32),
                pltpu.SemaphoreType.DMA((4, rows // (2 * TILE))),
            ],
        ),
        out_shape=[
            jax.ShapeDtypeStruct((rows, halo), BF),
            jax.ShapeDtypeStruct((rows, early - halo), BF),
            hbm((rows, n - early), BF),
            jax.ShapeDtypeStruct((rows, 3 * halo), BF),
            jax.ShapeDtypeStruct((rows, 4 * halo), BF),
            hbm((rows, TILE), F32),
        ],
        compiler_params=pltpu.CompilerParams(vmem_limit_bytes=24 << 20),
        name="mask_tiles",
    )(me, tile_mask, in_hbm(adj_local), in_hbm(adj_remote))


def gather_kernel(acc_ref, live_ref, *rest):
    parts, o_ref = rest[:-1], rest[-1]
    halo = parts[0].shape[0]
    total = acc_ref[...]
    for i, part in enumerate(parts):
        at = slice(i * halo, (i + 1) * halo)
        total = total + jnp.dot(live_ref[:, at], part[...], preferred_element_type=F32)
    o_ref[...] = total


def gather_halo(arrays, parts):
    rows = arrays[0].shape[0]
    hid = parts[0].shape[1]
    block = 256
    line = lambda w: pl.BlockSpec((block, w), lambda i: (i, 0))
    return pl.pallas_call(
        gather_kernel,
        grid=(rows // block,),
        in_specs=[line(a.shape[1]) for a in arrays] + [full(p.shape) for p in parts],
        out_specs=line(hid),
        out_shape=jax.ShapeDtypeStruct((rows, hid), F32),
        compiler_params=VM,
    )(*arrays, *parts)


def last_kernel(x_ref, w_ref, acc_ref, tail_hbm, scale_hbm, self_hbm, bias_ref, o_hbm,
                s_ref, h_ref, tail_ref, scale_ref, o_ref, sem):
    rows, hid = acc_ref.shape
    early, block = self_hbm.shape[0], 256
    ins = []
    for i in range(rows // block):
        at = pl.ds(i * block, block)
        some = [
            pltpu.make_async_copy(tail_hbm.at[at], tail_ref.at[at], sem.at[0, i]),
            pltpu.make_async_copy(scale_hbm.at[at], scale_ref.at[at], sem.at[2, i]),
        ]
        if i == 0:
            some.append(pltpu.make_async_copy(self_hbm, s_ref.at[pl.ds(0, early)], sem.at[3, 0]))
        for copy in some:
            copy.start()
        ins.append(some)
    first = (((0,), (0,)), ((), ()))
    for n0 in range(0, x_ref.shape[1], x_ref.shape[1]):
        at = slice(n0, n0 + x_ref.shape[1])
        both = lax.dot_general(x_ref[:, at], w_ref[...], first, preferred_element_type=F32)
        s_ref[pl.ds(early + at.start, at.stop - at.start), :] = both[:, :hid]
        h_ref[at, :] = both[:, hid:].astype(BF)
    outs = []
    for i in range(rows // block):
        for copy in ins[i]:
            copy.wait()
        at = slice(i * block, (i + 1) * block)
        more = jnp.dot(tail_ref[at, :], h_ref[...], preferred_element_type=F32)
        scale = jnp.concatenate([scale_ref[at, :]] * (hid // TILE), axis=1)
        o_ref[at, :] = jnp.maximum(
            s_ref[at, :] + (acc_ref[at, :] + more) * scale + bias_ref[...], 0.0
        ).astype(BF)
        at = pl.ds(i * block, block)
        outs.append(pltpu.make_async_copy(o_ref.at[at], o_hbm.at[at], sem.at[4, i]))
        outs[-1].start()
    for copy in outs:
        copy.wait()


def last_step(x, turned, acc, tail, scale, self_early, bias):
    rows, hid = acc.shape
    away = pl.BlockSpec(memory_space=pltpu.HBM)
    return pl.pallas_call(
        last_kernel,
        grid=(1,),
        in_specs=[full(x.shape), full(turned.shape), full(acc.shape)] + [away] * 3 + [full(bias.shape)],
        out_specs=away,
        scratch_shapes=[
            pltpu.VMEM((rows, hid), F32),
            pltpu.VMEM((x.shape[1], hid), BF),
            pltpu.VMEM(tail.shape, BF),
            pltpu.VMEM(scale.shape, F32),
            pltpu.VMEM((rows, hid), BF),
            pltpu.SemaphoreType.DMA((5, rows // 256)),
        ],
        out_shape=jax.ShapeDtypeStruct((rows, hid), BF),
        compiler_params=VM,
        name="last_step",
    )(x, turned, acc, *(in_hbm(a) for a in (tail, scale, self_early)), bias)


def shards(features, adj_local, adj_remote, tile_mask, w_self, w_neigh, out_bias):
    halo = adj_remote.shape[1] // (lax.axis_size("blk") - 1)
    me = lax.axis_index(("feat", "blk")).reshape(1)
    features = in_hbm(features)

    head, rest = split(me, features, EARLY)
    landed = [head[0]]
    for dz in range(1, NZ):
        landed.append(lax.ppermute(head[dz], "feat", feat_shift(dz, 0)))
    rest = lax.all_to_all(rest, "feat", split_axis=0, concat_axis=0, tiled=True)
    rest = rest.reshape(-1, rest.shape[-1])

    rot, turned = weights(me, w_self, w_neigh)
    live_head, live_mid, live_tail, live_near, live_far, scale = mask_tiles(
        me, tile_mask, adj_local, adj_remote, halo, EARLY
    )
    rows = regroup(landed, halo)
    parts, mids = [rows[0]], [rows[NX]]
    for j in range(1, NX):
        parts.append(lax.ppermute(rows[j], "feat", feat_shift(0, j)))
        mids.append(lax.ppermute(rows[NX + j], "feat", feat_shift(0, j)))
    h_head = halo_hidden(parts, rot, halo)
    same = []
    for dy in (1, 2, 3):
        same.append(lax.ppermute(h_head, "blk", blk_shift(dy, 0)))
    other = [lax.ppermute(h, "blk", blk_shift(0, 1)) for h in [h_head] + same]
    self_early, acc = mid_hidden(parts, mids, rot, h_head, live_head, live_mid)
    acc = gather_halo((acc, live_near), same)
    acc = gather_halo((acc, live_far), other)
    return last_step(rest, turned, acc, live_tail, scale, self_early, out_bias[None, :])


def solution(mesh):
    placed = (
        P("feat", None, "blk"),
        P(("feat", "blk"), None),
        P(("feat", "blk"), None),
        P(("feat", "blk"), None),
        P(),
        P(),
        P(),
    )

    return jax.shard_map(
        shards, mesh=mesh, in_specs=placed, out_specs=P(("feat", "blk"), None), check_vma=False
    )
```
